32 devices in a mesh: dom: 8 (over z, y), sub: 4 (over x, core).
Axes of the slice: x: 2, y: 2, z: 4, core: 2. Of those that a mesh axis runs over, the one named last changes fastest.
Arguments:
- start_basis: float32 [64, 16, 256, 128], P(None, 'sub', 'dom')
- stiffness: bfloat16 [16, 256, 4, 128, 128], P('sub', 'dom'), as said below
- pattern: int32 [16, 256, 4], P('sub', 'dom'), may hold values from 0 to 8, as said below
- lumped_mass: float32 [16, 256, 128], P('sub', 'dom'), may hold values from 0.5 to 2
Outputs:
- orthonormal_basis: float32 [64, 16, 256, 128], P(None, 'sub', 'dom')
- projected_operator: float32 [64, 64], replicated
The draws below stay inside these ranges and needn't reach their ends.
Inputs may be any that keep to these rules, and one draw needn't show every extreme that they name: `pattern`: slot 0 of every block row has offset 4, the block itself; the other slots of a row hold distinct offsets other than 4. `stiffness`: slot 0 blocks carry diagonal entries larger than their other entries.
All inputs are finite; a program needn't handle non-finite values.
Results may differ from the reference program's by a relative error of at most 0.0003.
Values sent between devices are 32-bit elements; how exact they have to be, the bound alone decides.
No kernel may reach another device: no remote copies, remote signals or barrier semaphores. Data moves between devices by JAX's collectives and lax.ppermute only.
A program may use at most 128 MiB of HBM per device.

```python
import math
import jax
import jax.numpy as jnp
from jax import lax

K = 64
BLOCK = 128
NNZ = 4
NBS = 16
NBD = 256


def draw_start_basis(key, part):
    first_key, second_key = jax.random.split(jax.random.fold_in(key, 11), 2)
    shape = (K, NBS, NBD, BLOCK)
    block_scale = jnp.exp(jax.random.uniform(second_key, (1, NBS, NBD, 1), jnp.float32, 0.0, 2.302585))
    values = jax.random.normal(first_key, shape, jnp.float32) * block_scale
    return values.astype(jnp.float32)


def draw_stiffness(key, part):
    subkey = jax.random.fold_in(key, 23)
    shape = (NBS, NBD, NNZ, BLOCK, BLOCK)
    noise = jax.random.normal(subkey, shape, jnp.float32)
    noise = noise / jnp.sqrt(jnp.float32(NNZ * BLOCK))
    centre = 2.5 * jnp.eye(BLOCK, dtype=jnp.float32)[None, :, :] * (jnp.arange(NNZ) == 0).astype(jnp.float32)[:, None, None]
    return (noise + centre[None, None]).astype(jnp.bfloat16)


def draw_pattern(key, part):
    subkey = jax.random.fold_in(key, 37)
    scores = jax.random.randint(subkey, (NBS, NBD, 8), 0, 1 << 20, dtype=jnp.int32) * 8 + jnp.arange(8, dtype=jnp.int32)
    ranking = jnp.argsort(scores, axis=-1, stable=True)[..., :NNZ - 1].astype(jnp.int32)
    others = jnp.where(ranking < 4, ranking, ranking + 1)
    centre = jnp.full((NBS, NBD, 1), 4, jnp.int32)
    return jnp.concatenate([centre, others], axis=-1).astype(jnp.int32)


def levels(key, dims, cuts, low, top_value):
    level = 1.0
    for axis_at, blocks in cuts:
        heights = jax.random.uniform(jax.random.fold_in(jax.random.fold_in(key, 6), axis_at), (blocks,), jnp.float32, low / len(cuts), top_value / len(cuts))
        level = level * jnp.repeat(jnp.exp(heights), dims[axis_at] // blocks).reshape((-1,) + (1,) * (len(dims) - 1 - axis_at))
    return level


def setup_inputs(seed: int = 0) -> dict:
    key_of = jax.random.split(jax.random.key(seed), 5)
    return {
        "start_basis": draw_start_basis(jax.random.fold_in(key_of[4], 71), 0),
        "stiffness": draw_stiffness(jax.random.fold_in(key_of[4], 71), 0),
        "pattern": draw_pattern(jax.random.fold_in(key_of[4], 71), 0),
        "lumped_mass": jnp.clip(jnp.exp(math.log(2.0) - 1.3862944 * jax.random.uniform(key_of[3], (NBS, NBD, BLOCK), jnp.float32) ** levels(key_of[3], (NBS, NBD, BLOCK), ((0, 4), (1, 8)), -0.2, 0.2)), 0.5, 2.0),
    }


HIGHEST = lax.Precision.HIGHEST

def couple(padded, stiffness, pattern):
    width_blocks = pattern.shape[1]

    def one_row(row_index):
        window = lax.dynamic_slice_in_dim(padded, row_index, 3, 1)
        offsets = lax.dynamic_index_in_dim(pattern, row_index, 0, False)
        blocks = lax.dynamic_index_in_dim(stiffness, row_index, 0, False).astype(jnp.float32)
        columns = jnp.arange(width_blocks, dtype=jnp.int32)[:, None] + offsets % 3
        picked = window[:, offsets // 3, columns, :]
        return jnp.einsum('djrc,kdjc->kdr', blocks, picked, precision=HIGHEST)
    rows_out = lax.map(one_row, jnp.arange(pattern.shape[0], dtype=jnp.int32))
    return jnp.transpose(rows_out, (1, 0, 2, 3))

def operate(coupled, field, lumped_mass):
    return (coupled / lumped_mass - 4.0 * field) / 3.0

def padding(field):
    return jnp.pad(field, ((0, 0), (1, 1), (1, 1), (0, 0)))

def reference(start_basis, stiffness, pattern, lumped_mass):
    level_one = operate(couple(padding(start_basis), stiffness, pattern), start_basis, lumped_mass)
    filtered = 2.0 * operate(couple(padding(level_one), stiffness, pattern), level_one, lumped_mass) - start_basis
    inverse_count = 1.0 / (NBS * NBD * BLOCK)
    gram_matrix = jnp.einsum('ksdr,lsdr->kl', filtered * lumped_mass, filtered, precision=HIGHEST) * inverse_count
    factor = jnp.linalg.cholesky(gram_matrix)
    flat = filtered.reshape(filtered.shape[0], -1)
    orthonormal = jax.scipy.linalg.solve_triangular(factor, flat, lower=True).reshape(filtered.shape)
    coupled = couple(padding(orthonormal), stiffness, pattern)
    projected = jnp.einsum('ksdr,lsdr->kl', orthonormal, coupled, precision=HIGHEST) * inverse_count
    return (orthonormal, projected)
```

```python
import functools

import jax
import jax.numpy as jnp
from jax import lax
from jax.experimental import pallas as pl
from jax.experimental.pallas import tpu as pltpu
from jax.sharding import PartitionSpec as P

F32 = jnp.float32
BF16 = jnp.bfloat16
UNROLL = 16

VMEM = pl.BlockSpec(memory_space=pltpu.VMEM)
SMEM = pl.BlockSpec(memory_space=pltpu.SMEM)
ANY = pl.BlockSpec(memory_space=pl.ANY)


def split(values):
    head = values.astype(BF16)
    rest = (values - head.astype(F32)).astype(BF16)
    return jnp.concatenate([head, rest], axis=0)


def joined(pair):
    wide = pair.astype(F32)
    half = wide.shape[0] // 2
    return wide[:half] + wide[half:]


def dot_last(left, right):
    return lax.dot_general(left, right, (((1,), (1,)), ((), ())), preferred_element_type=F32)


def folded(square):
    half = square.shape[0] // 2
    rows = square[:half] + square[half:]
    return rows[:, :half] + rows[:, half:]


class Grid:
    def __init__(self, rows, columns, flags=None):
        self.rows, self.columns, self.pitch = rows, columns, columns + 2
        self.blocks = (rows + 2) * self.pitch
        if flags is not None:
            lower, left = flags[0], flags[1]
            self.far_row = lower * (rows - 1)
            self.near_row = (1 - lower) * (rows - 1)
            self.far_halo = lower * (rows + 1)
            self.near_halo = (1 - lower) * (rows + 1)
            self.even_col = (1 - left) * (columns - 1)
            self.odd_col = left * (columns - 1)
            self.even_halo = (1 - left) * (columns + 1)
            self.odd_halo = left * (columns + 1)

    def own(self, row, column):
        return (row + 1) * self.pitch + column + 1

    def padded(self, row, column):
        return row * self.pitch + column

    def slot_rows(self):
        return [self.far_row, self.near_row] + list(range(1, self.rows - 1))


def prepare_kernel(rows, columns, flags, start, field, far, near, even, odd, staged, sems):
    grid = Grid(rows, columns, flags)
    k = far.shape[1]
    order = grid.slot_rows()

    def copy(slot):
        return pltpu.make_async_copy(start.at[:, order[slot]], staged.at[slot], sems.at[slot])

    for slot in range(rows):
        copy(slot).start()
    for slot in range(rows):
        copy(slot).wait()

        def body(step, _):
            for inner in range(8):
                column = step * 8 + inner
                values = staged[slot, :, pl.ds(step * 8, 8), :][:, inner, :]
                field[grid.own(order[slot], column)] = split(values)
                if slot == 0:
                    far[column] = values
                if slot == 1:
                    near[column] = values
            return 0

        lax.fori_loop(0, columns // 8, body, 0)
        even[slot] = joined(field[grid.own(order[slot], grid.even_col)])
        odd[slot] = joined(field[grid.own(order[slot], grid.odd_col)])


def prepare(flags, start):
    k, rows, columns, width = start.shape
    grid = Grid(rows, columns)
    edge = jax.ShapeDtypeStruct((columns, k, width), F32)
    side = jax.ShapeDtypeStruct((rows, k, width), F32)
    return pl.pallas_call(
        functools.partial(prepare_kernel, rows, columns),
        out_shape=(
            jax.ShapeDtypeStruct((grid.blocks, 2 * k, width), BF16),
            edge,
            edge,
            side,
            side,
        ),
        in_specs=[SMEM, ANY],
        out_specs=(VMEM,) * 5,
        scratch_shapes=[
            pltpu.VMEM((rows, k, columns, width), F32),
            pltpu.SemaphoreType.DMA((rows,)),
        ],
        compiler_params=pltpu.CompilerParams(vmem_limit_bytes=8 << 20),
    )(flags, start)


def level_kernel(level, part, rows, columns, *refs):
    refs = list(refs)
    flags, pattern, stiffness, mass, halo, corner = refs[:6]
    refs = refs[6:]
    sides = None
    if part == "near":
        sides, refs = refs[:2], refs[2:]
    base = None
    if level == 2:
        base, refs = refs[0], refs[1:]
    count = 1 if part == "near" else {1: 4, 2: 5, 3: 2}[level]
    refs = refs[count:]
    field, outs = refs[0], refs[1:]
    grid = Grid(rows, columns, flags)

    if part == "near":
        for slot, row in enumerate(grid.slot_rows()):
            field[grid.own(row, 0) - 1 + grid.even_halo] = split(sides[0][slot])
            field[grid.own(row, 0) - 1 + grid.odd_halo] = split(sides[1][slot])
        halo_row, first = grid.near_halo, 1
    else:
        halo_row, first = grid.far_halo, 0
    field[grid.padded(halo_row, grid.even_halo)] = split(corner[0])
    field[grid.padded(halo_row, grid.odd_halo)] = split(corner[1])

    def fill(step, _):
        for inner in range(8):
            column = step * 8 + inner
            field[grid.padded(halo_row, column + 1)] = split(halo[column])
        return 0

    lax.fori_loop(0, columns // 8, fill, 0)

    if level < 3:
        result, edge, even, odd = outs[:4]
    if level > 1:
        total = outs[-1]
        if part == "near":
            total[...] = jnp.zeros_like(total)

    groups = columns // UNROLL
    lines = rows - 1 if part == "near" else 1

    def body(step, _):
        line = step // groups
        start = (step % groups) * UNROLL
        if part == "near":
            row = jnp.where(line == lines - 1, grid.near_row, line + 1)
        else:
            row = grid.far_row
        lefts, rights = [], []
        for inner in range(UNROLL):
            column = start + inner
            corner_index = grid.padded(row, column)
            blocks = []
            for slot in range(4):
                if slot == 0:
                    index = grid.own(row, column)
                else:
                    offset = pattern[(row * columns + column) * 4 + slot]
                    index = corner_index + offset + (grid.pitch - 3) * ((offset * 11) >> 5)
                blocks.append(field[index])
            own_pair = blocks[0]
            values = jnp.concatenate(blocks, axis=1)
            matrix = jnp.concatenate([stiffness[row, column, slot] for slot in range(4)], axis=1)
            products = dot_last(values, matrix)
            half = products.shape[0] // 2
            coupled = products[:half] + products[half:]
            if level == 3:
                lefts.append(own_pair)
                rights.append(split(coupled))
            else:
                weight = mass[row, pl.ds(column, 1), :]
                scaled = coupled * (1.0 / (3.0 * weight)) - (4.0 / 3.0) * joined(own_pair)
                if level == 2:
                    scaled = 2.0 * scaled - joined(base[grid.own(row, column)])
                pair = split(scaled)
                result[grid.own(row, column)] = pair
                edge[column] = scaled
                if level == 2:
                    lefts.append(split(scaled * weight))
                    rights.append(pair)
        if level > 1:
            sums = None
            for at in range(0, UNROLL, 4):
                term = dot_last(
                    jnp.concatenate(lefts[at : at + 4], axis=1),
                    jnp.concatenate(rights[at : at + 4], axis=1),
                )
                sums = term if sums is None else sums + term
            total[...] += folded(sums)
        return 0

    lax.fori_loop(0, lines * groups, body, 0)

    if level < 3:
        slots = enumerate(grid.slot_rows())
        for slot, row in slots:
            if (slot == 0) == (part == "far"):
                even[slot] = joined(result[grid.own(row, grid.even_col)])
                odd[slot] = joined(result[grid.own(row, grid.odd_col)])


def level_call(level, part, operands, sides, base, state):
    flags, pattern, stiffness, mass, halo, corner = operands
    columns, k, width = halo.shape
    rows = stiffness.shape[0]
    grid = Grid(rows, columns)
    pair = jax.ShapeDtypeStruct((grid.blocks, 2 * k, width), BF16)
    edge = jax.ShapeDtypeStruct((columns, k, width), F32)
    side = jax.ShapeDtypeStruct((rows, k, width), F32)
    square = jax.ShapeDtypeStruct((k, k), F32)
    outs = [pair]
    if level < 3:
        outs += [pair, edge, side, side]
    if level > 1:
        outs.append(square)
    args = list(operands) + list(sides) + ([base] if level == 2 else [])
    first = len(args)
    if part == "near":
        aliases = {first: 0}
    else:
        where = {1: [0, 1, 3, 4], 2: [0, 1, 3, 4, 5], 3: [0, 1]}[level]
        aliases = {first + at: out for at, out in enumerate(where)}
    args += list(state)
    specs = [SMEM, SMEM] + [VMEM] * (len(args) - 2)
    return pl.pallas_call(
        functools.partial(level_kernel, level, part, rows, columns),
        out_shape=tuple(outs),
        in_specs=specs,
        out_specs=(VMEM,) * len(outs),
        input_output_aliases=aliases,
        compiler_params=pltpu.CompilerParams(vmem_limit_bytes=4 << 20),
        name=f"level{level}_{part}",
    )(*args)


def finish_kernel(rows, columns, inverse_count, sums, field, out, projected, staged, sems):
    k = projected.shape[0]
    grid = Grid(rows, columns)
    highest = lax.Precision.HIGHEST
    lanes = lax.broadcasted_iota(jnp.int32, (k, 2 * k), 1)
    lines = lax.broadcasted_iota(jnp.int32, (k, 2 * k), 0)
    gram = sums[:, :k] * inverse_count
    work = jnp.concatenate([gram, (lines == lanes).astype(F32)[:, :k]], axis=1)
    scales = jnp.zeros((k, 1), F32)
    for at in range(k):
        pivot = work[at : at + 1, at : at + 1]
        line = work[at : at + 1, :]
        column = work[:, at : at + 1] * (1.0 / pivot)
        below = lines[:, :1] > at
        work = work - jnp.where(below, column, 0.0) * line
        scales = jnp.where(lines[:, :1] == at, lax.rsqrt(pivot), scales)
    inverse = work[:, k:] * scales
    moments = sums[:, k:] * inverse_count
    half = jnp.dot(inverse, moments, precision=highest, preferred_element_type=F32)
    projected[...] = lax.dot_general(
        half, inverse, (((1,), (1,)), ((), ())), precision=highest, preferred_element_type=F32
    )
    parts = split(inverse)
    left = jnp.concatenate([parts, parts], axis=1)

    def copy(row, slot):
        return pltpu.make_async_copy(staged.at[slot], out.at[:, row], sems.at[slot])

    for row in range(rows):
        slot = row % 2
        if row >= 2:
            copy(row - 2, slot).wait()

        def body(step, _):
            blocks = []
            for inner in range(8):
                column = step * 8 + inner
                both = jnp.dot(left, field[grid.own(row, column)], preferred_element_type=F32)
                blocks.append((both[:k] + both[k:])[:, None, :])
            staged[slot, :, pl.ds(step * 8, 8), :] = jnp.concatenate(blocks, axis=1)
            return 0

        lax.fori_loop(0, columns // 8, body, 0)
        copy(row, slot).start()
    for row in range(max(rows - 2, 0), rows):
        copy(row, row % 2).wait()


def finish(sums, field, rows, columns, inverse_count):
    k = sums.shape[0]
    width = field.shape[2]
    return pl.pallas_call(
        functools.partial(finish_kernel, rows, columns, inverse_count),
        out_shape=(
            jax.ShapeDtypeStruct((k, rows, columns, width), F32),
            jax.ShapeDtypeStruct((k, k), F32),
        ),
        in_specs=[VMEM, VMEM],
        out_specs=(ANY, VMEM),
        scratch_shapes=[
            pltpu.VMEM((2, k, columns, width), F32),
            pltpu.SemaphoreType.DMA((2,)),
        ],
        compiler_params=pltpu.CompilerParams(vmem_limit_bytes=8 << 20),
    )(sums, field)


def swap(values, axis, first):
    count = lax.axis_size(axis)
    pairs = []
    for i in range(first, count - 1, 2):
        pairs += [(i, i + 1), (i + 1, i)]
    return lax.ppermute(values, axis, pairs)


def summed(values, axis):
    count = lax.axis_size(axis)
    if count & (count - 1):
        return lax.psum(values, axis)
    bit = 1
    while bit < count:
        values = values + lax.ppermute(values, axis, [(i, i ^ bit) for i in range(count)])
        bit *= 2
    return values


def on_device(start_basis, stiffness, pattern, lumped_mass):
    k, rows, columns, width = start_basis.shape
    flags = jnp.stack([lax.axis_index("sub") % 2, lax.axis_index("dom") % 2]).astype(jnp.int32)
    pattern = pattern.reshape(-1)
    field, far, near, even, odd = prepare(flags, start_basis)
    base = field
    total = None
    for level in (1, 2, 3):
        got_far = swap(far, "sub", 1)
        got_near = swap(near, "sub", 0)
        got_even = swap(even, "dom", 0)
        got_odd = swap(odd, "dom", 1)
        near_corner = swap(jnp.concatenate([got_even[1:2], got_odd[1:2]]), "sub", 0)
        far_corner = swap(jnp.concatenate([got_even[0:1], got_odd[0:1]]), "sub", 1)
        shared = (flags, pattern, stiffness, lumped_mass)
        outs = level_call(
            level, "near", shared + (got_near, near_corner), (got_even, got_odd), base, (field,)
        )
        if level == 1:
            field, result, near, even, odd = outs
            state = (field, result, even, odd)
        elif level == 2:
            field, result, near, even, odd, total = outs
            state = (field, result, even, odd, total)
        else:
            field, moments = outs
            state = (field, moments)
        outs = level_call(level, "far", shared + (got_far, far_corner), (), base, state)
        if level == 1:
            base, field, far, even, odd = outs
        elif level == 2:
            _, field, far, even, odd, total = outs
        else:
            field, moments = outs
    sums = jnp.concatenate([total, moments], axis=1)
    for axis in ("sub", "dom"):
        sums = summed(sums, axis)
    vertex_count = rows * columns * width * lax.axis_size("dom") * lax.axis_size("sub")
    return finish(sums, field, rows, columns, 1.0 / vertex_count)


def solution(mesh):
    in_specs = (
        P(None, "sub", "dom", None),
        P("sub", "dom", None, None, None),
        P("sub", "dom", None),
        P("sub", "dom", None),
    )
    out_specs = (P(None, "sub", "dom", None), P())
    return jax.shard_map(
        on_device, mesh=mesh, in_specs=in_specs, out_specs=out_specs, check_vma=False
    )
```

```python
import functools

import jax
import jax.numpy as jnp
from jax import lax
from jax.experimental import pallas as pl
from jax.experimental.pallas import tpu as pltpu
from jax.sharding import PartitionSpec as P

F32 = jnp.float32
BF16 = jnp.bfloat16

VMEM = pl.BlockSpec(memory_space=pltpu.VMEM)
SMEM = pl.BlockSpec(memory_space=pltpu.SMEM)
HBM = pl.BlockSpec(memory_space=pltpu.HBM)


def split(values):
    head = values.astype(BF16)
    rest = (values - head.astype(F32)).astype(BF16)
    return jnp.concatenate([head, rest], axis=0)


def joined(pair):
    wide = pair.astype(F32)
    half = wide.shape[0] // 2
    return wide[:half] + wide[half:]


def placed(values, space):
    return pltpu.with_memory_space_constraint(values, space)


def dot_last(left, right):
    return lax.dot_general(left, right, (((1,), (1,)), ((), ())), preferred_element_type=F32)


def folded(square):
    half = square.shape[0] // 2
    rows = square[:half] + square[half:]
    return rows[:, :half] + rows[:, half:]


class Grid:
    def __init__(self, rows, columns, flags=None):
        self.rows, self.columns, self.pitch = rows, columns, columns + 2
        self.blocks = (rows + 2) * self.pitch
        if flags is not None:
            lower, left = flags[0], flags[1]
            self.far_row = lower * (rows - 1)
            self.near_row = (1 - lower) * (rows - 1)
            self.far_halo = lower * (rows + 1)
            self.near_halo = (1 - lower) * (rows + 1)
            self.even_col = (1 - left) * (columns - 1)
            self.odd_col = left * (columns - 1)
            self.even_halo = (1 - left) * (columns + 1)
            self.odd_halo = left * (columns + 1)

    def own(self, row, column):
        return (row + 1) * self.pitch + column + 1

    def padded(self, row, column):
        return row * self.pitch + column

    def slot_rows(self):
        return [self.far_row, self.near_row] + list(range(1, self.rows - 1))


def prepare_kernel(
    rows, columns, flags, start, mass, far, near, even, odd, held, staged, ends, sems, mass_sem
):
    grid = Grid(rows, columns, flags)
    order = grid.slot_rows()
    left, right = 0, columns - 8
    holding = pltpu.make_async_copy(mass, held, mass_sem)

    def copies(slot):
        if slot < 2:
            return [pltpu.make_async_copy(start.at[:, order[slot]], staged.at[slot], sems.at[slot])]
        return [
            pltpu.make_async_copy(
                start.at[:, order[slot], pl.ds(first, 8)],
                ends.at[2 * slot - 4 + side],
                sems.at[2 * slot - 2 + side],
            )
            for side, first in enumerate((left, right))
        ]

    for slot in range(rows):
        for copy in copies(slot):
            copy.start()
    holding.start()
    for slot, edge in ((0, far), (1, near)):
        for copy in copies(slot):
            copy.wait()

        def body(step, _):
            first = pl.multiple_of(step * 8, 8)
            tile = pltpu.einshape("kdr->dkr", staged[slot, :, pl.ds(first, 8), :])
            for inner in range(8):
                edge[step * 8 + inner] = tile[inner]
            return 0

        lax.fori_loop(0, columns // 8, body, 0)
        even[slot] = edge[grid.even_col]
        odd[slot] = edge[grid.odd_col]
    even_right = grid.even_col > 0
    for slot in range(2, rows):
        for copy in copies(slot):
            copy.wait()
        first = pltpu.einshape("kdr->dkr", ends[2 * slot - 4])[0]
        last = pltpu.einshape("kdr->dkr", ends[2 * slot - 3])[7]
        even[slot] = jnp.where(even_right, last, first)
        odd[slot] = jnp.where(even_right, first, last)
    holding.wait()


def prepare(flags, start, mass):
    k, rows, columns, width = start.shape
    edge = jax.ShapeDtypeStruct((columns, k, width), F32)
    side = jax.ShapeDtypeStruct((rows, k, width), F32)
    return pl.pallas_call(
        functools.partial(prepare_kernel, rows, columns),
        out_shape=(edge, edge, side, side, pltpu.VMEM(mass.shape, F32)),
        in_specs=[SMEM, HBM, HBM],
        out_specs=(VMEM,) * 5,
        scratch_shapes=[
            pltpu.VMEM((2, k, columns, width), F32),
            pltpu.VMEM((2 * rows - 4, k, 8, width), F32),
            pltpu.SemaphoreType.DMA((2 * rows - 2,)),
            pltpu.SemaphoreType.DMA(()),
        ],
        compiler_params=pltpu.CompilerParams(vmem_limit_bytes=6 << 20),
        name="prepare",
    )(flags, placed(start, pltpu.HBM), placed(mass, pltpu.HBM))


def corners_kernel(mark, even_side, odd_side, far_corner, near_corner):
    for slot, corner in enumerate((far_corner, near_corner)):
        corner[0] = even_side[slot]
        corner[1] = odd_side[slot]


def corners(mark, even_side, odd_side):
    shape = jax.ShapeDtypeStruct((2,) + even_side.shape[1:], F32)
    return pl.pallas_call(
        corners_kernel,
        out_shape=(shape, shape),
        in_specs=[SMEM, VMEM, VMEM],
        out_specs=(VMEM, VMEM),
        compiler_params=pltpu.CompilerParams(vmem_limit_bytes=1 << 20),
        name="corners",
    )(mark, even_side, odd_side)


def stride_of(count):
    return max(size for size in range(1, 17) if count % size == 0)


def level_kernel(level, part, rows, columns, ref):
    grid = Grid(rows, columns, ref["flags"])
    pattern, mass = ref["pattern"], ref["mass"]
    total = ref.get("total")
    base = ref["outer"]
    field = ref["middle"] if level == 2 else ref["outer"]
    result = {1: ref.get("middle"), 2: ref["outer"], 3: None}[level]
    stiffness = ref["loaded"] if "loaded" in ref else ref["stiffness"]
    order = grid.slot_rows()

    loads = {}
    if "loaded" in ref:
        wanted = {"inner": order[2:] + order[1:2], "near": order[:1]}[part]
        half = columns // 2
        for at, row in enumerate(wanted):
            for side in range(2):
                piece = (row, pl.ds(side * half, half))
                loads[at, side] = pltpu.make_async_copy(
                    ref["stiffness"].at[piece],
                    ref["loaded"].at[piece],
                    ref["load_sems"].at[2 * at + side],
                )
    if level == 1 and part == "inner":
        fetches = [
            pltpu.make_async_copy(
                ref["start"].at[:, order[slot]], ref["staged"].at[slot - 2], ref["sems"].at[slot - 2]
            )
            for slot in range(2, rows)
        ]
        for fetch in fetches:
            fetch.start()
    for load in loads.values():
        load.start()

    def fill(row, blocks):
        def body(step, _):
            for inner in range(8):
                column = step * 8 + inner
                field[grid.padded(row, column + 1)] = split(blocks[column])
            return 0

        lax.fori_loop(0, columns // 8, body, 0)

    if level == 1 and part == "inner":
        fill(grid.far_row + 1, ref["far_edge"])
        fill(grid.near_row + 1, ref["near_edge"])
        for slot in range(2, rows):
            fetches[slot - 2].wait()

            def relay(step, _):
                first = pl.multiple_of(step * 8, 8)
                values = ref["staged"][slot - 2, :, pl.ds(first, 8), :]
                tile = pltpu.einshape("kdr->dkr", values)
                for inner in range(8):
                    field[grid.own(order[slot], step * 8 + inner)] = split(tile[inner])
                return 0

            lax.fori_loop(0, columns // 8, relay, 0)
    if part == "near":
        for slot, row in enumerate(order):
            field[grid.padded(row + 1, grid.even_halo)] = split(ref["even_side"][slot])
            field[grid.padded(row + 1, grid.odd_halo)] = split(ref["odd_side"][slot])
        fill(grid.near_halo, ref["near_halo"])
    if part == "far":
        for row, name in ((grid.far_halo, "far_corner"), (grid.near_halo, "near_corner")):
            field[grid.padded(row, grid.even_halo)] = split(ref[name][0])
            field[grid.padded(row, grid.odd_halo)] = split(ref[name][1])
        fill(grid.far_halo, ref["far_halo"])

    def block(row, column, edge):
        corner = grid.padded(row, column)
        own = grid.own(row, column)
        blocks = [field[own]]
        for slot in range(1, 4):
            offset = pattern[row, slot, column]
            blocks.append(field[corner + offset + (grid.pitch - 3) * ((offset * 11) >> 5)])
        matrix = jnp.concatenate([stiffness[row, column, slot] for slot in range(4)], axis=1)
        products = dot_last(jnp.concatenate(blocks, axis=1), matrix)
        half = products.shape[0] // 2
        coupled = products[:half] + products[half:]
        if level == 3:
            return blocks[0], split(coupled)
        weight = mass[row, pl.ds(column, 1), :]
        scaled = coupled * (1.0 / (3.0 * weight)) - (4.0 / 3.0) * joined(blocks[0])
        if level == 2:
            scaled = 2.0 * scaled - joined(base[own])
        pair = split(scaled)
        result[own] = pair
        if edge is not None:
            edge[column] = scaled
        return (split(scaled * weight), pair) if level == 2 else (None, None)

    def add_terms(terms):
        if level == 1:
            return
        sums = None
        for at in range(0, len(terms), 4):
            lefts, rights = zip(*terms[at : at + 4])
            term = dot_last(jnp.concatenate(lefts, axis=1), jnp.concatenate(rights, axis=1))
            sums = term if sums is None else sums + term
        total[...] += folded(sums)

    def sweep(row, first, count, edge):
        size = stride_of(count)

        def body(step, _):
            add_terms([block(row, first + step * size + at, edge) for at in range(size)])
            return 0

        lax.fori_loop(0, count // size, body, 0)

    near_edge = ref.get("near_edge") if level < 3 else None
    if part == "inner":
        ref["mark"][0] = 0
        if level > 1:
            total[...] = jnp.zeros_like(total)
        size = stride_of(columns - 2)
        groups = (columns - 2) // size
        for (at, side), load in loads.items():
            if at < rows - 2:
                load.wait()

        def body(step, _):
            row = 1 + step // groups
            first = 1 + (step % groups) * size
            add_terms([block(row, first + at, None) for at in range(size)])
            return 0

        lax.fori_loop(0, (rows - 2) * groups, body, 0)
        for (at, side), load in loads.items():
            if at >= rows - 2:
                load.wait()
    ends = (0, columns - 1)
    if part == "near":
        sweep(grid.near_row, 1, columns - 2, near_edge)
        add_terms([block(row, column, None) for row in order[2:] for column in ends])
        for load in loads.values():
            load.wait()
    if part == "far":
        sweep(grid.far_row, 0, columns, ref.get("far_edge") if level < 3 else None)
        add_terms([block(grid.near_row, column, near_edge) for column in ends])
    if level < 3 and part != "inner":
        for slot, row in enumerate(order):
            if (slot < 2) == (part == "far"):
                ref["even"][slot] = joined(result[grid.own(row, grid.even_col)])
                ref["odd"][slot] = joined(result[grid.own(row, grid.odd_col)])


def level_call(level, part, values):
    columns, k, width = values["near_edge"].shape
    rows = values["mass"].shape[0]
    grid = Grid(rows, columns)
    edge = jax.ShapeDtypeStruct((columns, k, width), F32)
    side = jax.ShapeDtypeStruct((rows, k, width), F32)
    pair = pltpu.VMEM((grid.blocks, 2 * k, width), BF16)
    shapes = {
        "outer": pair,
        "middle": pair,
        "far_edge": edge,
        "near_edge": edge,
        "even": side,
        "odd": side,
        "mark": jax.ShapeDtypeStruct((1,), jnp.int32),
        "total": jax.ShapeDtypeStruct((k, k), F32),
        "loaded": pltpu.VMEM(values["stiffness"].shape, BF16),
    }
    read = ["flags", "pattern", "mass"]
    updated, made = [], []
    if level == 1 and part != "far":
        read.append("stiffness")
        (made if part == "inner" else updated).append("loaded")
    else:
        read.append("loaded")
    (made if (level, part) == (1, "inner") else updated).extend(
        ["outer", "middle"] if level < 3 else ["outer"]
    )
    if level > 1:
        (made if part == "inner" else updated).append("total")
    scratch = {}
    if part == "inner":
        made.append("mark")
        if level == 1:
            read += ["start", "far_edge", "near_edge"]
            scratch["staged"] = pltpu.VMEM((rows - 2, k, columns, width), F32)
            scratch["sems"] = pltpu.SemaphoreType.DMA((rows - 2,))
            scratch["load_sems"] = pltpu.SemaphoreType.DMA((2 * rows - 2,))
    elif part == "near":
        read += ["even_side", "odd_side", "near_halo"]
        made += ["near_edge", "even", "odd"] if level < 3 else []
        if level == 1:
            scratch["load_sems"] = pltpu.SemaphoreType.DMA((2,))
    else:
        read += ["far_corner", "near_corner", "far_halo"]
        updated += ["near_edge", "even", "odd"] if level < 3 else []
        made += ["far_edge"] if level < 3 else []
    specs = {"flags": SMEM, "pattern": SMEM, "mark": SMEM, "stiffness": HBM, "start": HBM}
    spaces = dict.fromkeys(("outer", "middle", "loaded", "mass"), pltpu.VMEM)
    spaces.update(stiffness=pltpu.HBM, start=pltpu.HBM)

    def kernel(*refs):
        skipped = len(read) + len(updated)
        names = read + updated + made + list(scratch)
        ref = dict(zip(names, refs[: len(read)] + refs[skipped:]))
        if "loaded" in read:
            ref["stiffness"] = ref.pop("loaded")
        level_kernel(level, part, rows, columns, ref)

    outs = pl.pallas_call(
        kernel,
        out_shape=tuple(shapes[name] for name in updated + made),
        in_specs=[specs.get(name, VMEM) for name in read + updated],
        out_specs=tuple(specs.get(name, VMEM) for name in updated + made),
        scratch_shapes=list(scratch.values()),
        input_output_aliases={len(read) + at: at for at in range(len(updated))},
        compiler_params=pltpu.CompilerParams(vmem_limit_bytes=6 << 20),
        name=f"level{level}_{part}",
    )(*[placed(values[name], spaces[name]) if name in spaces else values[name]
        for name in read + updated])
    return {**values, **dict(zip(updated + made, outs))}


def finish_kernel(rows, columns, inverse_count, sums, field, out, projected, staged, sems):
    k = projected.shape[0]
    grid = Grid(rows, columns)
    highest = lax.Precision.HIGHEST
    lanes = lax.broadcasted_iota(jnp.int32, (k, 2 * k), 1)
    lines = lax.broadcasted_iota(jnp.int32, (k, 2 * k), 0)
    gram = sums[:, :k] * inverse_count
    work = jnp.concatenate([gram, (lines == lanes).astype(F32)[:, :k]], axis=1)
    scales = jnp.zeros((k, 1), F32)
    for at in range(k):
        pivot = work[at : at + 1, at : at + 1]
        line = work[at : at + 1, :]
        column = work[:, at : at + 1] * (1.0 / pivot)
        below = lines[:, :1] > at
        work = work - jnp.where(below, column, 0.0) * line
        scales = jnp.where(lines[:, :1] == at, lax.rsqrt(pivot), scales)
    inverse = work[:, k:] * scales
    moments = sums[:, k:] * inverse_count
    half = jnp.dot(inverse, moments, precision=highest, preferred_element_type=F32)
    projected[...] = lax.dot_general(
        half, inverse, (((1,), (1,)), ((), ())), precision=highest, preferred_element_type=F32
    )
    parts = split(inverse)
    left = jnp.concatenate([parts, parts], axis=1)

    def copy(row, slot):
        return pltpu.make_async_copy(staged.at[slot], out.at[:, row], sems.at[slot])

    for row in range(rows):
        slot = row % 2
        if row >= 2:
            copy(row - 2, slot).wait()

        def body(step, _):
            blocks = []
            for inner in range(8):
                column = step * 8 + inner
                both = jnp.dot(left, field[grid.own(row, column)], preferred_element_type=F32)
                blocks.append((both[:k] + both[k:])[None])
            tile = pltpu.einshape("dkr->kdr", jnp.concatenate(blocks, axis=0))
            staged[slot, :, pl.ds(pl.multiple_of(step * 8, 8), 8), :] = tile
            return 0

        lax.fori_loop(0, columns // 8, body, 0)
        copy(row, slot).start()
    for row in range(max(rows - 2, 0), rows):
        copy(row, row % 2).wait()


def finish(sums, field, rows, columns, inverse_count):
    k = sums.shape[0]
    width = field.shape[2]
    return pl.pallas_call(
        functools.partial(finish_kernel, rows, columns, inverse_count),
        out_shape=(
            jax.ShapeDtypeStruct((k, rows, columns, width), F32),
            jax.ShapeDtypeStruct((k, k), F32),
        ),
        in_specs=[VMEM, VMEM],
        out_specs=(HBM, VMEM),
        scratch_shapes=[
            pltpu.VMEM((2, k, columns, width), F32),
            pltpu.SemaphoreType.DMA((2,)),
        ],
        compiler_params=pltpu.CompilerParams(vmem_limit_bytes=8 << 20),
        name="finish",
    )(sums, placed(field, pltpu.VMEM))


def swap(values, axis, first):
    count = lax.axis_size(axis)
    pairs = []
    for i in range(first, count - 1, 2):
        pairs += [(i, i + 1), (i + 1, i)]
    return lax.ppermute(values, axis, pairs)


def summed(values, axis):
    count = lax.axis_size(axis)
    if count & (count - 1):
        return lax.psum(values, axis)
    bit = 1
    while bit < count:
        values = values + lax.ppermute(values, axis, [(i, i ^ bit) for i in range(count)])
        bit *= 2
    return values


def on_device(start_basis, stiffness, pattern, lumped_mass):
    k, rows, columns, width = start_basis.shape
    flags = jnp.stack([lax.axis_index("sub") % 2, lax.axis_index("dom") % 2]).astype(jnp.int32)
    values = {
        "flags": flags,
        "pattern": jnp.transpose(pattern, (0, 2, 1)),
        "stiffness": stiffness,
        "start": start_basis,
    }
    made = prepare(flags, start_basis, lumped_mass)
    values.update(zip(("far_edge", "near_edge", "even", "odd", "mass"), made))
    totals = []
    for level in (1, 2, 3):
        values["far_halo"] = swap(values["far_edge"], "sub", 1)
        values["near_halo"] = swap(values["near_edge"], "sub", 0)
        values["even_side"] = swap(values["even"], "dom", 0)
        values["odd_side"] = swap(values["odd"], "dom", 1)
        values = level_call(level, "inner", values)
        far_corner, near_corner = corners(
            values["mark"], values["even_side"], values["odd_side"]
        )
        values["far_corner"] = swap(far_corner, "sub", 1)
        values["near_corner"] = swap(near_corner, "sub", 0)
        values = level_call(level, "near", values)
        values = level_call(level, "far", values)
        if level > 1:
            totals.append(values["total"])
    sums = jnp.concatenate(totals, axis=1)
    for axis in ("sub", "dom"):
        sums = summed(sums, axis)
    vertex_count = rows * columns * width * lax.axis_size("dom") * lax.axis_size("sub")
    return finish(sums, values["outer"], rows, columns, 1.0 / vertex_count)


def solution(mesh):
    in_specs = (
        P(None, "sub", "dom", None),
        P("sub", "dom", None, None, None),
        P("sub", "dom", None),
        P("sub", "dom", None),
    )
    out_specs = (P(None, "sub", "dom", None), P())
    return jax.shard_map(
        on_device, mesh=mesh, in_specs=in_specs, out_specs=out_specs, check_vma=False
    )
```

```python
import functools

import jax
import jax.numpy as jnp
from jax import lax
from jax.experimental import pallas as pl
from jax.experimental.pallas import tpu as pltpu
from jax.sharding import PartitionSpec as P

F32 = jnp.float32
BF16 = jnp.bfloat16
LONGEST = 32

VMEM = pl.BlockSpec(memory_space=pltpu.VMEM)
SMEM = pl.BlockSpec(memory_space=pltpu.SMEM)
HBM = pl.BlockSpec(memory_space=pltpu.HBM)


def split(values):
    head = values.astype(BF16)
    rest = (values - head.astype(F32)).astype(BF16)
    return jnp.concatenate([head, rest], axis=0)


def joined(pair):
    wide = pair.astype(F32)
    half = wide.shape[0] // 2
    return wide[:half] + wide[half:]


def placed(values, space):
    return pltpu.with_memory_space_constraint(values, space)


def dot_last(left, right):
    return lax.dot_general(left, right, (((1,), (1,)), ((), ())), preferred_element_type=F32)


def folded(square):
    half = square.shape[0] // 2
    rows = square[:half] + square[half:]
    return rows[:, :half] + rows[:, half:]


class Grid:
    def __init__(self, rows, columns, flags=None):
        self.rows, self.columns, self.pitch = rows, columns, columns + 2
        self.blocks = (rows + 2) * self.pitch
        if flags is not None:
            lower, left = flags[0], flags[1]
            self.lower, self.left = lower, left
            self.far_row = lower * (rows - 1)
            self.near_row = (1 - lower) * (rows - 1)
            self.far_halo = lower * (rows + 1)
            self.near_halo = (1 - lower) * (rows + 1)
            self.even_col = (1 - left) * (columns - 1)
            self.odd_col = left * (columns - 1)
            self.even_halo = (1 - left) * (columns + 1)
            self.odd_halo = left * (columns + 1)

    def own(self, row, column):
        return (row + 1) * self.pitch + column + 1

    def padded(self, row, column):
        return row * self.pitch + column

    def slot_rows(self):
        return [self.far_row, self.near_row] + list(range(1, self.rows - 1))


def prepare_kernel(
    rows, columns, flags, start, mass, pattern, far, near, even, odd, held_mass, held_pattern,
    staged, ends, sems, held_sems
):
    grid = Grid(rows, columns, flags)
    order = grid.slot_rows()
    left, right = 0, columns - 8
    holds = [
        pltpu.make_async_copy(mass, held_mass, held_sems.at[0]),
        pltpu.make_async_copy(pattern, held_pattern, held_sems.at[1]),
    ]

    def copies(slot):
        if slot < 2:
            return [pltpu.make_async_copy(start.at[:, order[slot]], staged.at[slot], sems.at[slot])]
        return [
            pltpu.make_async_copy(
                start.at[:, order[slot], pl.ds(first, 8)],
                ends.at[2 * slot - 4 + side],
                sems.at[2 * slot - 2 + side],
            )
            for side, first in enumerate((left, right))
        ]

    for slot in range(rows):
        for copy in copies(slot):
            copy.start()
    for hold in holds:
        hold.start()
    for slot, edge in ((0, far), (1, near)):
        for copy in copies(slot):
            copy.wait()

        def body(step, _):
            first = pl.multiple_of(step * 8, 8)
            tile = pltpu.einshape("kdr->dkr", staged[slot, :, pl.ds(first, 8), :])
            for inner in range(8):
                edge[step * 8 + inner] = tile[inner]
            return 0

        lax.fori_loop(0, columns // 8, body, 0)
        even[slot] = edge[grid.even_col]
        odd[slot] = edge[grid.odd_col]
    even_right = grid.even_col > 0
    for slot in range(2, rows):
        for copy in copies(slot):
            copy.wait()
        first = pltpu.einshape("kdr->dkr", ends[2 * slot - 4])[0]
        last = pltpu.einshape("kdr->dkr", ends[2 * slot - 3])[7]
        even[slot] = jnp.where(even_right, last, first)
        odd[slot] = jnp.where(even_right, first, last)
    for hold in holds:
        hold.wait()


def prepare(flags, start, mass, pattern):
    k, rows, columns, width = start.shape
    edge = jax.ShapeDtypeStruct((columns, k, width), F32)
    side = jax.ShapeDtypeStruct((rows, k, width), F32)
    return pl.pallas_call(
        functools.partial(prepare_kernel, rows, columns),
        out_shape=(
            edge,
            edge,
            side,
            side,
            pltpu.VMEM(mass.shape, F32),
            pltpu.VMEM(pattern.shape, jnp.int32),
        ),
        in_specs=[SMEM, HBM, HBM, HBM],
        out_specs=(VMEM,) * 6,
        scratch_shapes=[
            pltpu.VMEM((2, k, columns, width), F32),
            pltpu.VMEM((2 * rows - 4, k, 8, width), F32),
            pltpu.SemaphoreType.DMA((2 * rows - 2,)),
            pltpu.SemaphoreType.DMA((2,)),
        ],
        compiler_params=pltpu.CompilerParams(vmem_limit_bytes=6 << 20),
        name="prepare",
    )(flags, *(placed(values, pltpu.HBM) for values in (start, mass, pattern)))


def corners_kernel(mark, even_side, odd_side, far_corner, near_corner):
    for slot, corner in enumerate((far_corner, near_corner)):
        corner[0] = even_side[slot]
        corner[1] = odd_side[slot]


def corners(mark, even_side, odd_side):
    shape = jax.ShapeDtypeStruct((2,) + even_side.shape[1:], F32)
    return pl.pallas_call(
        corners_kernel,
        out_shape=(shape, shape),
        in_specs=[SMEM, VMEM, VMEM],
        out_specs=(VMEM, VMEM),
        compiler_params=pltpu.CompilerParams(vmem_limit_bytes=1 << 20),
        name="corners",
    )(mark, even_side, odd_side)


def stride_of(count):
    return max(size for size in range(1, LONGEST + 1) if count % size == 0)


def level_kernel(level, part, rows, columns, ref):
    grid = Grid(rows, columns, ref["flags"])
    pattern, mass = ref["pattern"], ref["mass"]
    total = ref.get("total")
    base = ref["outer"]
    field = ref["middle"] if level == 2 else ref["outer"]
    result = {1: ref.get("middle"), 2: ref["outer"], 3: None}[level]
    stiffness = ref["loaded"] if "loaded" in ref else ref["stiffness"]
    order = grid.slot_rows()

    loads, ahead = 0, 3
    if "loaded" in ref:
        half = columns // 2

        def load(at):
            row = grid.far_row
            if part == "inner":
                row = jnp.where(at // 2 < rows - 2, 1 + at // 2, grid.near_row)
            piece = (row, pl.ds(at % 2 * half, half))
            return pltpu.make_async_copy(
                ref["stiffness"].at[piece], ref["loaded"].at[piece], ref["load_sems"].at[at]
            )

        loads = 2 * rows - 2 if part == "inner" else 2
    if level == 1 and part == "inner":
        fetches = [
            pltpu.make_async_copy(
                ref["start"].at[:, order[slot]], ref["staged"].at[slot - 2], ref["sems"].at[slot - 2]
            )
            for slot in range(2, rows)
        ]
        for fetch in fetches:
            fetch.start()
    if part == "near":
        for at in range(loads):
            load(at).start()

    def fill(row, blocks):
        def body(step, _):
            for inner in range(8):
                column = step * 8 + inner
                field[grid.padded(row, column + 1)] = split(blocks[column])
            return 0

        lax.fori_loop(0, columns // 8, body, 0)

    if level == 1 and part == "inner":
        fill(grid.far_row + 1, ref["far_edge"])
        fill(grid.near_row + 1, ref["near_edge"])
        for fetch in fetches:
            fetch.wait()
        for at in range(ahead):
            load(at).start()
        for slot in range(2, rows):

            def relay(step, _):
                first = pl.multiple_of(step * 8, 8)
                values = ref["staged"][slot - 2, :, pl.ds(first, 8), :]
                tile = pltpu.einshape("kdr->dkr", values)
                for inner in range(8):
                    field[grid.own(order[slot], step * 8 + inner)] = split(tile[inner])
                return 0

            lax.fori_loop(0, columns // 8, relay, 0)
    if part == "near":
        for slot, row in enumerate(order):
            field[grid.padded(row + 1, grid.even_halo)] = split(ref["even_side"][slot])
            field[grid.padded(row + 1, grid.odd_halo)] = split(ref["odd_side"][slot])
        fill(grid.near_halo, ref["near_halo"])
    if part == "far":
        for row, name in ((grid.far_halo, "far_corner"), (grid.near_halo, "near_corner")):
            for at, halo in enumerate((grid.even_halo, grid.odd_halo)):
                if level == 3:
                    field[grid.padded(row, halo)] = jnp.zeros(field.shape[1:], BF16)
                else:
                    field[grid.padded(row, halo)] = split(ref[name][at])
        fill(grid.far_halo, ref["far_halo"])

    def block(row, column, edge):
        corner = grid.padded(row, column)
        own = grid.own(row, column)
        blocks = [field[own]]
        for slot in range(1, 4):
            offset = pattern[row, slot, column]
            blocks.append(field[corner + offset + (grid.pitch - 3) * ((offset * 11) >> 5)])
        matrix = jnp.concatenate([stiffness[row, column, slot] for slot in range(4)], axis=1)
        products = dot_last(jnp.concatenate(blocks, axis=1), matrix)
        half = products.shape[0] // 2
        coupled = products[:half] + products[half:]
        if level == 3:
            return blocks[0], split(coupled)
        weight = mass[row, pl.ds(column, 1), :]
        scaled = coupled * (1.0 / (3.0 * weight)) - (4.0 / 3.0) * joined(blocks[0])
        if level == 2:
            scaled = 2.0 * scaled - joined(base[own])
        pair = split(scaled)
        result[own] = pair
        if edge is not None:
            edge[column] = scaled
        return (split(scaled * weight), pair) if level == 2 else (None, None)

    def add_terms(terms):
        if level == 1:
            return
        sums = None
        for at in range(0, len(terms), 4):
            lefts, rights = zip(*terms[at : at + 4])
            term = dot_last(jnp.concatenate(lefts, axis=1), jnp.concatenate(rights, axis=1))
            sums = term if sums is None else sums + term
        total[...] += folded(sums)

    def sweep(row, first, count, edge):
        size = stride_of(count)

        def body(step, _):
            add_terms([block(row, first + step * size + at, edge) for at in range(size)])
            return 0

        lax.fori_loop(0, count // size, body, 0)

    near_edge = ref.get("near_edge") if level < 3 else None
    if part == "inner":
        ref["mark"][0] = 0
        if level > 1:
            total[...] = jnp.zeros_like(total)
        size = (columns - 2) // 2 if level == 1 else stride_of(columns - 2)
        groups = (columns - 2) // size

        def body(step, _):
            row = 1 + step // groups
            first = 1 + (step % groups) * size
            if loads:
                load(step).wait()

                @pl.when(step + ahead < loads)
                def _():
                    load(step + ahead).start()

            add_terms([block(row, first + at, None) for at in range(size)])
            return 0

        lax.fori_loop(0, (rows - 2) * groups, body, 0)
        if loads:
            for at in range(2 * rows - 4 + ahead, loads):
                load(at).start()
            for at in range(2 * rows - 4, loads):
                load(at).wait()
    ends = (0, columns - 1)
    if part == "near":
        sweep(grid.near_row, 1, columns - 2, near_edge)
        add_terms([block(row, column, None) for row in order[2:] for column in ends])
        for at in range(loads):
            load(at).wait()
    if part == "far":
        sweep(grid.far_row, 0, columns, ref.get("far_edge") if level < 3 else None)
        add_terms([block(grid.near_row, column, near_edge) for column in ends])
    if level == 3 and part != "inner":
        slot = rows + (part == "near")
        halo = ref["near_halo"] if part == "near" else ref["far_halo"]
        for name, column in (("even_side", grid.even_col), ("odd_side", grid.odd_col)):
            total[...] += folded(dot_last(split(ref[name][slot]), split(halo[column])))
    if level == 2 and part == "far":
        for slot, row in enumerate(order[:2]):
            down = grid.lower * 2 - 1 if slot == 0 else 1 - grid.lower * 2
            for name, column, right in (
                ("even", grid.even_col, 1 - grid.left * 2),
                ("odd", grid.odd_col, grid.left * 2 - 1),
            ):
                across = 3 * (down + 1) + right + 1
                matrix = jnp.zeros(stiffness.shape[3:], BF16)
                for at in range(1, 4):
                    hit = pattern[row, at, column] == across
                    matrix = jnp.where(hit, stiffness[row, column, at], matrix)
                values = jnp.dot(
                    result[grid.own(row, column)], matrix, preferred_element_type=F32
                )
                half = values.shape[0] // 2
                ref[name][rows + slot] = values[:half] + values[half:]
    if level < 3 and part != "inner":
        for slot, row in enumerate(order):
            if (slot < 2) == (part == "far"):
                ref["even"][slot] = joined(result[grid.own(row, grid.even_col)])
                ref["odd"][slot] = joined(result[grid.own(row, grid.odd_col)])


def level_call(level, part, values):
    columns, k, width = values["near_edge"].shape
    rows = values["mass"].shape[0]
    grid = Grid(rows, columns)
    edge = jax.ShapeDtypeStruct((columns, k, width), F32)
    side = jax.ShapeDtypeStruct((rows + 2 * (level == 2), k, width), F32)
    pair = pltpu.VMEM((grid.blocks, 2 * k, width), BF16)
    shapes = {
        "outer": pair,
        "middle": pair,
        "far_edge": edge,
        "near_edge": edge,
        "even": side,
        "odd": side,
        "mark": jax.ShapeDtypeStruct((1,), jnp.int32),
        "total": jax.ShapeDtypeStruct((k, k), F32),
        "loaded": pltpu.VMEM(values["stiffness"].shape, BF16),
    }
    read = ["flags", "pattern", "mass"]
    updated, made = [], []
    if level == 1 and part != "far":
        read.append("stiffness")
        (made if part == "inner" else updated).append("loaded")
    else:
        read.append("loaded")
    (made if (level, part) == (1, "inner") else updated).extend(
        ["outer", "middle"] if level < 3 else ["outer"]
    )
    if level > 1:
        (made if part == "inner" else updated).append("total")
    scratch = {}
    if part == "inner":
        made.append("mark")
        if level == 1:
            read += ["start", "far_edge", "near_edge"]
            scratch["staged"] = pltpu.VMEM((rows - 2, k, columns, width), F32)
            scratch["sems"] = pltpu.SemaphoreType.DMA((rows - 2,))
            scratch["load_sems"] = pltpu.SemaphoreType.DMA((2 * rows - 2,))
    elif part == "near":
        read += ["even_side", "odd_side", "near_halo"]
        made += ["near_edge", "even", "odd"] if level < 3 else []
        if level == 1:
            scratch["load_sems"] = pltpu.SemaphoreType.DMA((2,))
    else:
        read.append("far_halo")
        read += ["far_corner", "near_corner"] if level < 3 else ["even_side", "odd_side"]
        updated += ["near_edge", "even", "odd"] if level < 3 else []
        made += ["far_edge"] if level < 3 else []
    specs = {"flags": SMEM, "pattern": SMEM, "mark": SMEM, "stiffness": HBM, "start": HBM}
    spaces = dict.fromkeys(("outer", "middle", "loaded", "mass", "pattern"), pltpu.VMEM)
    spaces.update(stiffness=pltpu.HBM, start=pltpu.HBM)

    def kernel(*refs):
        skipped = len(read) + len(updated)
        names = read + updated + made + list(scratch)
        ref = dict(zip(names, refs[: len(read)] + refs[skipped:]))
        if "loaded" in read:
            ref["stiffness"] = ref.pop("loaded")
        level_kernel(level, part, rows, columns, ref)

    outs = pl.pallas_call(
        kernel,
        out_shape=tuple(shapes[name] for name in updated + made),
        in_specs=[specs.get(name, VMEM) for name in read + updated],
        out_specs=tuple(specs.get(name, VMEM) for name in updated + made),
        scratch_shapes=list(scratch.values()),
        input_output_aliases={len(read) + at: at for at in range(len(updated))},
        compiler_params=pltpu.CompilerParams(vmem_limit_bytes=6 << 20),
        name=f"level{level}_{part}",
    )(*[placed(values[name], spaces[name]) if name in spaces else values[name]
        for name in read + updated])
    return {**values, **dict(zip(updated + made, outs))}


def inverse_factor(gram):
    k, step = gram.shape[0], 8
    lines = lax.broadcasted_iota(jnp.int32, (k, 2 * k), 0)
    lanes = lax.broadcasted_iota(jnp.int32, (k, 2 * k), 1)
    work = jnp.concatenate([gram, (lines == lanes).astype(F32)[:, :k]], axis=1)
    finished = []
    for first in range(0, k, step):
        rows = [work[at : at + 1] for at in range(step)]
        columns = [
            jnp.broadcast_to(work[:, first + at : first + at + 1], work.shape)
            for at in range(step)
        ]
        entries = [
            [jnp.broadcast_to(rows[i][:, first + j : first + j + 1], (1, 2 * k)) for j in range(step)]
            for i in range(step)
        ]
        change = None
        for i in range(step):
            scale = 1.0 / entries[i][i]
            line = rows[i] * scale
            for j in range(i + 1, step):
                factor = entries[i][j] * scale
                for t in range(j, step):
                    entries[j][t] = entries[j][t] - factor * entries[i][t]
                rows[j] = rows[j] - factor * rows[i]
                columns[j] = columns[j] - columns[i] * factor
            column = jnp.where(lines[:step] > i, columns[i][:step], 0.0)
            if work.shape[0] > step:
                column = jnp.concatenate([column, columns[i][step:]], axis=0)
            change = column * line if change is None else change + column * line
        work = work - change
        finished.append(work[:step])
        work = work[step:]
    work = jnp.concatenate(finished, axis=0)
    pivots = jnp.sum(jnp.where(lines == lanes, work, 0.0), axis=1, keepdims=True)
    return work[:, k:] * lax.rsqrt(pivots)


def finish_kernel(rows, columns, inverse_count, sums, field, out, projected, staged, sems):
    k = projected.shape[0]
    grid = Grid(rows, columns)
    highest = lax.Precision.HIGHEST
    inverse = inverse_factor(sums[:, :k] * inverse_count)
    moments = sums[:, k:] * inverse_count
    half = jnp.dot(inverse, moments, precision=highest, preferred_element_type=F32)
    projected[...] = lax.dot_general(
        half, inverse, (((1,), (1,)), ((), ())), precision=highest, preferred_element_type=F32
    )
    parts = split(inverse)
    left = jnp.concatenate([parts, parts], axis=1)

    def copy(row, slot):
        return pltpu.make_async_copy(staged.at[slot], out.at[:, row], sems.at[slot])

    for row in range(rows):
        slot = row % 2
        if row >= 2:
            copy(row - 2, slot).wait()

        def body(step, _):
            blocks = []
            for inner in range(8):
                column = step * 8 + inner
                both = jnp.dot(left, field[grid.own(row, column)], preferred_element_type=F32)
                blocks.append((both[:k] + both[k:])[None])
            tile = pltpu.einshape("dkr->kdr", jnp.concatenate(blocks, axis=0))
            staged[slot, :, pl.ds(pl.multiple_of(step * 8, 8), 8), :] = tile
            return 0

        lax.fori_loop(0, columns // 8, body, 0)
        copy(row, slot).start()
    for row in range(max(rows - 2, 0), rows):
        copy(row, row % 2).wait()


def finish(sums, field, rows, columns, inverse_count):
    k = sums.shape[0]
    width = field.shape[2]
    return pl.pallas_call(
        functools.partial(finish_kernel, rows, columns, inverse_count),
        out_shape=(
            jax.ShapeDtypeStruct((k, rows, columns, width), F32),
            jax.ShapeDtypeStruct((k, k), F32),
        ),
        in_specs=[VMEM, VMEM],
        out_specs=(HBM, VMEM),
        scratch_shapes=[
            pltpu.VMEM((2, k, columns, width), F32),
            pltpu.SemaphoreType.DMA((2,)),
        ],
        compiler_params=pltpu.CompilerParams(vmem_limit_bytes=8 << 20),
        name="finish",
    )(sums, placed(field, pltpu.VMEM))


def swap(values, axis, first):
    count = lax.axis_size(axis)
    pairs = []
    for i in range(first, count - 1, 2):
        pairs += [(i, i + 1), (i + 1, i)]
    return lax.ppermute(values, axis, pairs)


def summed(values, axis):
    count = lax.axis_size(axis)
    if count & (count - 1):
        return lax.psum(values, axis)
    bit = 1
    while bit < count:
        values = values + lax.ppermute(values, axis, [(i, i ^ bit) for i in range(count)])
        bit *= 2
    return values


def on_device(start_basis, stiffness, pattern, lumped_mass):
    k, rows, columns, width = start_basis.shape
    flags = jnp.stack([lax.axis_index("sub") % 2, lax.axis_index("dom") % 2]).astype(jnp.int32)
    values = {
        "flags": flags,
        "stiffness": stiffness,
        "start": start_basis,
    }
    made = prepare(flags, start_basis, lumped_mass, jnp.transpose(pattern, (0, 2, 1)))
    values.update(zip(("far_edge", "near_edge", "even", "odd", "mass", "pattern"), made))
    totals = []
    for level in (1, 2, 3):
        values["far_halo"] = swap(values["far_edge"], "sub", 1)
        values["near_halo"] = swap(values["near_edge"], "sub", 0)
        values["even_side"] = swap(values["even"], "dom", 0)
        values["odd_side"] = swap(values["odd"], "dom", 1)
        values = level_call(level, "inner", values)
        if level < 3:
            far_corner, near_corner = corners(
                values["mark"], values["even_side"], values["odd_side"]
            )
            values["far_corner"] = swap(far_corner, "sub", 1)
            values["near_corner"] = swap(near_corner, "sub", 0)
        values = level_call(level, "near", values)
        values = level_call(level, "far", values)
        if level > 1:
            totals.append(values["total"])
    sums = jnp.concatenate(totals, axis=1)
    for axis in ("sub", "dom"):
        sums = summed(sums, axis)
    vertex_count = rows * columns * width * lax.axis_size("dom") * lax.axis_size("sub")
    return finish(sums, values["outer"], rows, columns, 1.0 / vertex_count)


def solution(mesh):
    in_specs = (
        P(None, "sub", "dom", None),
        P("sub", "dom", None, None, None),
        P("sub", "dom", None),
        P("sub", "dom", None),
    )
    out_specs = (P(None, "sub", "dom", None), P())
    return jax.shard_map(
        on_device, mesh=mesh, in_specs=in_specs, out_specs=out_specs, check_vma=False
    )
```

```python
import functools

import jax
import jax.numpy as jnp
from jax import lax
from jax.experimental import pallas as pl
from jax.experimental.pallas import tpu as pltpu
from jax.sharding import PartitionSpec as P

F32 = jnp.float32
BF16 = jnp.bfloat16
LONGEST = 32

VMEM = pl.BlockSpec(memory_space=pltpu.VMEM)
SMEM = pl.BlockSpec(memory_space=pltpu.SMEM)
HBM = pl.BlockSpec(memory_space=pltpu.HBM)


(
    FLAGS, PATTERN, MASS, STIFFNESS, LOADED, OUTER, MIDDLE, TOTAL, FAR_EDGE, NEAR_EDGE, EVEN, ODD,
    MARK, START, STAGED, SEMS, LOAD_SEMS, EVEN_SIDE, ODD_SIDE, NEAR_HALO, FAR_HALO, FAR_CORNER,
    NEAR_CORNER,
) = range(23)
INNER, NEAR, FAR = range(3)


def split(values):
    head = values.astype(BF16)
    rest = (values - head.astype(F32)).astype(BF16)
    return jnp.concatenate([head, rest], axis=0)


def joined(pair):
    wide = pair.astype(F32)
    half = wide.shape[0] // 2
    return wide[:half] + wide[half:]


def placed(values, space):
    return pltpu.with_memory_space_constraint(values, space)


def dot_last(left, right):
    return lax.dot_general(left, right, (((1,), (1,)), ((), ())), preferred_element_type=F32)


def folded(square):
    half = square.shape[0] // 2
    rows = square[:half] + square[half:]
    return rows[:, :half] + rows[:, half:]


class Grid:
    def __init__(self, rows, columns, flags=None):
        self.rows, self.columns, self.pitch = rows, columns, columns + 2
        self.blocks = (rows + 2) * self.pitch
        if flags is not None:
            lower, left = flags[0], flags[1]
            self.lower, self.left = lower, left
            self.far_row = lower * (rows - 1)
            self.near_row = (1 - lower) * (rows - 1)
            self.far_halo = lower * (rows + 1)
            self.near_halo = (1 - lower) * (rows + 1)
            self.even_col = (1 - left) * (columns - 1)
            self.odd_col = left * (columns - 1)
            self.even_halo = (1 - left) * (columns + 1)
            self.odd_halo = left * (columns + 1)

    def own(self, row, column):
        return (row + 1) * self.pitch + column + 1

    def padded(self, row, column):
        return row * self.pitch + column

    def slot_rows(self):
        return [self.far_row, self.near_row] + list(range(1, self.rows - 1))


def prepare_kernel(
    rows, columns, flags, start, mass, pattern, far, near, even, odd, held_mass, held_pattern,
    staged, ends, sems, held_sems
):
    grid = Grid(rows, columns, flags)
    order = grid.slot_rows()
    left, right = 0, columns - 8
    holds = [
        pltpu.make_async_copy(mass, held_mass, held_sems.at[0]),
        pltpu.make_async_copy(pattern, held_pattern, held_sems.at[1]),
    ]

    def copies(slot):
        if slot < 2:
            return [pltpu.make_async_copy(start.at[:, order[slot]], staged.at[slot], sems.at[slot])]
        return [
            pltpu.make_async_copy(
                start.at[:, order[slot], pl.ds(first, 8)],
                ends.at[2 * slot - 4 + side],
                sems.at[2 * slot - 2 + side],
            )
            for side, first in enumerate((left, right))
        ]

    for slot in range(rows):
        for copy in copies(slot):
            copy.start()
    for hold in holds:
        hold.start()
    for slot, edge in ((0, far), (1, near)):
        for copy in copies(slot):
            copy.wait()

        def body(step, _):
            first = pl.multiple_of(step * 8, 8)
            tile = pltpu.einshape("kdr->dkr", staged[slot, :, pl.ds(first, 8), :])
            for inner in range(8):
                edge[step * 8 + inner] = tile[inner]
            return 0

        lax.fori_loop(0, columns // 8, body, 0)
        even[slot] = edge[grid.even_col]
        odd[slot] = edge[grid.odd_col]
    even_right = grid.even_col > 0
    for slot in range(2, rows):
        for copy in copies(slot):
            copy.wait()
        first = pltpu.einshape("kdr->dkr", ends[2 * slot - 4])[0]
        last = pltpu.einshape("kdr->dkr", ends[2 * slot - 3])[7]
        even[slot] = jnp.where(even_right, last, first)
        odd[slot] = jnp.where(even_right, first, last)
    for hold in holds:
        hold.wait()


def prepare(flags, start, mass, pattern):
    k, rows, columns, width = start.shape
    edge = jax.ShapeDtypeStruct((columns, k, width), F32)
    side = jax.ShapeDtypeStruct((rows, k, width), F32)
    return pl.pallas_call(
        functools.partial(prepare_kernel, rows, columns),
        out_shape=(
            edge,
            edge,
            side,
            side,
            pltpu.VMEM(mass.shape, F32),
            pltpu.VMEM(pattern.shape, jnp.int32),
        ),
        in_specs=[SMEM, HBM, HBM, HBM],
        out_specs=(VMEM,) * 6,
        scratch_shapes=[
            pltpu.VMEM((2, k, columns, width), F32),
            pltpu.VMEM((2 * rows - 4, k, 8, width), F32),
            pltpu.SemaphoreType.DMA((2 * rows - 2,)),
            pltpu.SemaphoreType.DMA((2,)),
        ],
        compiler_params=pltpu.CompilerParams(vmem_limit_bytes=6 << 20),
        name="prepare",
    )(flags, *(placed(values, pltpu.HBM) for values in (start, mass, pattern)))


def corners_kernel(mark, even_side, odd_side, far_corner, near_corner):
    for slot, corner in enumerate((far_corner, near_corner)):
        corner[0] = even_side[slot]
        corner[1] = odd_side[slot]


def corners(mark, even_side, odd_side):
    shape = jax.ShapeDtypeStruct((2,) + even_side.shape[1:], F32)
    return pl.pallas_call(
        corners_kernel,
        out_shape=(shape, shape),
        in_specs=[SMEM, VMEM, VMEM],
        out_specs=(VMEM, VMEM),
        compiler_params=pltpu.CompilerParams(vmem_limit_bytes=1 << 20),
        name="corners",
    )(mark, even_side, odd_side)


def stride_of(count):
    return max(size for size in range(1, LONGEST + 1) if count % size == 0)


def level_kernel(level, part, rows, columns, ref):
    grid = Grid(rows, columns, ref[FLAGS])
    pattern, mass = ref[PATTERN], ref[MASS]
    total = ref.get(TOTAL)
    base = ref[OUTER]
    field = ref[MIDDLE] if level == 2 else ref[OUTER]
    result = {1: ref.get(MIDDLE), 2: ref[OUTER], 3: None}[level]
    stiffness = ref[LOADED] if LOADED in ref else ref[STIFFNESS]
    order = grid.slot_rows()

    loads, ahead = 0, 3
    if LOADED in ref:
        half = columns // 2

        def load(at):
            row = grid.far_row
            if part == INNER:
                row = jnp.where(at // 2 < rows - 2, 1 + at // 2, grid.near_row)
            piece = (row, pl.ds(at % 2 * half, half))
            return pltpu.make_async_copy(
                ref[STIFFNESS].at[piece], ref[LOADED].at[piece], ref[LOAD_SEMS].at[at]
            )

        loads = 2 * rows - 2 if part == INNER else 2
    if level == 1 and part == INNER:
        fetches = [
            pltpu.make_async_copy(
                ref[START].at[:, order[slot]], ref[STAGED].at[slot - 2], ref[SEMS].at[slot - 2]
            )
            for slot in range(2, rows)
        ]
        for fetch in fetches:
            fetch.start()
    if part == NEAR:
        for at in range(loads):
            load(at).start()

    def fill(row, blocks):
        def body(step, _):
            for inner in range(8):
                column = step * 8 + inner
                field[grid.padded(row, column + 1)] = split(blocks[column])
            return 0

        lax.fori_loop(0, columns // 8, body, 0)

    if level == 1 and part == INNER:
        fill(grid.far_row + 1, ref[FAR_EDGE])
        fill(grid.near_row + 1, ref[NEAR_EDGE])
        for fetch in fetches:
            fetch.wait()
        for at in range(ahead):
            load(at).start()
        for slot in range(2, rows):

            def relay(step, _):
                first = pl.multiple_of(step * 8, 8)
                values = ref[STAGED][slot - 2, :, pl.ds(first, 8), :]
                tile = pltpu.einshape("kdr->dkr", values)
                for inner in range(8):
                    field[grid.own(order[slot], step * 8 + inner)] = split(tile[inner])
                return 0

            lax.fori_loop(0, columns // 8, relay, 0)
    if part == NEAR:
        for slot, row in enumerate(order):
            field[grid.padded(row + 1, grid.even_halo)] = split(ref[EVEN_SIDE][slot])
            field[grid.padded(row + 1, grid.odd_halo)] = split(ref[ODD_SIDE][slot])
        fill(grid.near_halo, ref[NEAR_HALO])
    if part == FAR:
        for row, name in ((grid.far_halo, FAR_CORNER), (grid.near_halo, NEAR_CORNER)):
            for at, halo in enumerate((grid.even_halo, grid.odd_halo)):
                if level == 3:
                    field[grid.padded(row, halo)] = jnp.zeros(field.shape[1:], BF16)
                else:
                    field[grid.padded(row, halo)] = split(ref[name][at])
        fill(grid.far_halo, ref[FAR_HALO])

    def block(row, column, edge):
        corner = grid.padded(row, column)
        own = grid.own(row, column)
        blocks = [field[own]]
        for slot in range(1, 4):
            offset = pattern[row, slot, column]
            blocks.append(field[corner + offset + (grid.pitch - 3) * ((offset * 11) >> 5)])
        matrix = jnp.concatenate([stiffness[row, column, slot] for slot in range(4)], axis=1)
        products = dot_last(jnp.concatenate(blocks, axis=1), matrix)
        half = products.shape[0] // 2
        coupled = products[:half] + products[half:]
        if level == 3:
            return blocks[0], split(coupled)
        weight = mass[row, pl.ds(column, 1), :]
        scaled = coupled * (1.0 / (3.0 * weight)) - (4.0 / 3.0) * joined(blocks[0])
        if level == 2:
            scaled = 2.0 * scaled - joined(base[own])
        pair = split(scaled)
        result[own] = pair
        if edge is not None:
            edge[column] = scaled
        return (split(scaled * weight), pair) if level == 2 else (None, None)

    def add_terms(terms):
        if level == 1:
            return
        sums = None
        for at in range(0, len(terms), 4):
            lefts, rights = zip(*terms[at : at + 4])
            term = dot_last(jnp.concatenate(lefts, axis=1), jnp.concatenate(rights, axis=1))
            sums = term if sums is None else sums + term
        total[...] += folded(sums)

    def sweep(row, first, count, edge):
        size = stride_of(count)

        def body(step, _):
            add_terms([block(row, first + step * size + at, edge) for at in range(size)])
            return 0

        lax.fori_loop(0, count // size, body, 0)

    near_edge = ref.get(NEAR_EDGE) if level < 3 else None
    if part == INNER:
        ref[MARK][0] = 0
        if level > 1:
            total[...] = jnp.zeros_like(total)
        size = (columns - 2) // 2 if level == 1 else stride_of(columns - 2)
        groups = (columns - 2) // size

        def body(step, _):
            row = 1 + step // groups
            first = 1 + (step % groups) * size
            if loads:
                load(step).wait()

                @pl.when(step + ahead < loads)
                def _():
                    load(step + ahead).start()

            add_terms([block(row, first + at, None) for at in range(size)])
            return 0

        lax.fori_loop(0, (rows - 2) * groups, body, 0)
        if loads:
            for at in range(2 * rows - 4 + ahead, loads):
                load(at).start()
            for at in range(2 * rows - 4, loads):
                load(at).wait()
    ends = (0, columns - 1)
    if part == NEAR:
        sweep(grid.near_row, 1, columns - 2, near_edge)
        add_terms([block(row, column, None) for row in order[2:] for column in ends])
        for at in range(loads):
            load(at).wait()
    if part == FAR:
        sweep(grid.far_row, 0, columns, ref.get(FAR_EDGE) if level < 3 else None)
        add_terms([block(grid.near_row, column, near_edge) for column in ends])
    if level == 3 and part != INNER:
        slot = rows + (part == NEAR)
        halo = ref[NEAR_HALO] if part == NEAR else ref[FAR_HALO]
        for name, column in ((EVEN_SIDE, grid.even_col), (ODD_SIDE, grid.odd_col)):
            total[...] += folded(dot_last(split(ref[name][slot]), split(halo[column])))
    if level == 2 and part == FAR:
        for slot, row in enumerate(order[:2]):
            down = grid.lower * 2 - 1 if slot == 0 else 1 - grid.lower * 2
            for name, column, right in (
                (EVEN, grid.even_col, 1 - grid.left * 2),
                (ODD, grid.odd_col, grid.left * 2 - 1),
            ):
                across = 3 * (down + 1) + right + 1
                matrix = jnp.zeros(stiffness.shape[3:], BF16)
                for at in range(1, 4):
                    hit = pattern[row, at, column] == across
                    matrix = jnp.where(hit, stiffness[row, column, at], matrix)
                values = jnp.dot(
                    result[grid.own(row, column)], matrix, preferred_element_type=F32
                )
                half = values.shape[0] // 2
                ref[name][rows + slot] = values[:half] + values[half:]
    if level < 3 and part != INNER:
        for slot, row in enumerate(order):
            if (slot < 2) == (part == FAR):
                ref[EVEN][slot] = joined(result[grid.own(row, grid.even_col)])
                ref[ODD][slot] = joined(result[grid.own(row, grid.odd_col)])


def level_call(level, part, values):
    columns, k, width = values[NEAR_EDGE].shape
    rows = values[MASS].shape[0]
    grid = Grid(rows, columns)
    edge = jax.ShapeDtypeStruct((columns, k, width), F32)
    side = jax.ShapeDtypeStruct((rows + 2 * (level == 2), k, width), F32)
    pair = pltpu.VMEM((grid.blocks, 2 * k, width), BF16)
    shapes = {
        OUTER: pair,
        MIDDLE: pair,
        FAR_EDGE: edge,
        NEAR_EDGE: edge,
        EVEN: side,
        ODD: side,
        MARK: jax.ShapeDtypeStruct((1,), jnp.int32),
        TOTAL: jax.ShapeDtypeStruct((k, k), F32),
        LOADED: pltpu.VMEM(values[STIFFNESS].shape, BF16),
    }
    read = [FLAGS, PATTERN, MASS]
    updated, made = [], []
    if level == 1 and part != FAR:
        read.append(STIFFNESS)
        (made if part == INNER else updated).append(LOADED)
    else:
        read.append(LOADED)
    (made if (level, part) == (1, INNER) else updated).extend(
        [OUTER, MIDDLE] if level < 3 else [OUTER]
    )
    if level > 1:
        (made if part == INNER else updated).append(TOTAL)
    scratch = {}
    if part == INNER:
        made.append(MARK)
        if level == 1:
            read += [START, FAR_EDGE, NEAR_EDGE]
            scratch[STAGED] = pltpu.VMEM((rows - 2, k, columns, width), F32)
            scratch[SEMS] = pltpu.SemaphoreType.DMA((rows - 2,))
            scratch[LOAD_SEMS] = pltpu.SemaphoreType.DMA((2 * rows - 2,))
    elif part == NEAR:
        read += [EVEN_SIDE, ODD_SIDE, NEAR_HALO]
        made += [NEAR_EDGE, EVEN, ODD] if level < 3 else []
        if level == 1:
            scratch[LOAD_SEMS] = pltpu.SemaphoreType.DMA((2,))
    else:
        read.append(FAR_HALO)
        read += [FAR_CORNER, NEAR_CORNER] if level < 3 else [EVEN_SIDE, ODD_SIDE]
        updated += [NEAR_EDGE, EVEN, ODD] if level < 3 else []
        made += [FAR_EDGE] if level < 3 else []
    specs = {FLAGS: SMEM, PATTERN: SMEM, MARK: SMEM, STIFFNESS: HBM, START: HBM}
    spaces = dict.fromkeys((OUTER, MIDDLE, LOADED, MASS, PATTERN), pltpu.VMEM)
    spaces.update({STIFFNESS: pltpu.HBM, START: pltpu.HBM})

    def kernel(*refs):
        skipped = len(read) + len(updated)
        names = read + updated + made + list(scratch)
        ref = dict(zip(names, refs[: len(read)] + refs[skipped:]))
        if LOADED in read:
            ref[STIFFNESS] = ref.pop(LOADED)
        level_kernel(level, part, rows, columns, ref)

    outs = pl.pallas_call(
        kernel,
        out_shape=tuple(shapes[name] for name in updated + made),
        in_specs=[specs.get(name, VMEM) for name in read + updated],
        out_specs=tuple(specs.get(name, VMEM) for name in updated + made),
        scratch_shapes=list(scratch.values()),
        input_output_aliases={len(read) + at: at for at in range(len(updated))},
        compiler_params=pltpu.CompilerParams(vmem_limit_bytes=6 << 20),
        name=("inner", "near", "far")[part],
    )(*[placed(values[name], spaces[name]) if name in spaces else values[name]
        for name in read + updated])
    return {**values, **dict(zip(updated + made, outs))}


def inverse_factor(gram):
    k, step = gram.shape[0], 8
    lines = lax.broadcasted_iota(jnp.int32, (k, 2 * k), 0)
    lanes = lax.broadcasted_iota(jnp.int32, (k, 2 * k), 1)
    work = jnp.concatenate([gram, (lines == lanes).astype(F32)[:, :k]], axis=1)
    finished = []
    for first in range(0, k, step):
        rows = [work[at : at + 1] for at in range(step)]
        columns = [
            jnp.broadcast_to(work[:, first + at : first + at + 1], work.shape)
            for at in range(step)
        ]
        entries = [
            [jnp.broadcast_to(rows[i][:, first + j : first + j + 1], (1, 2 * k)) for j in range(step)]
            for i in range(step)
        ]
        change = None
        for i in range(step):
            scale = 1.0 / entries[i][i]
            line = rows[i] * scale
            for j in range(i + 1, step):
                factor = entries[i][j] * scale
                for t in range(j, step):
                    entries[j][t] = entries[j][t] - factor * entries[i][t]
                rows[j] = rows[j] - factor * rows[i]
                columns[j] = columns[j] - columns[i] * factor
            column = jnp.where(lines[:step] > i, columns[i][:step], 0.0)
            if work.shape[0] > step:
                column = jnp.concatenate([column, columns[i][step:]], axis=0)
            change = column * line if change is None else change + column * line
        work = work - change
        finished.append(work[:step])
        work = work[step:]
    work = jnp.concatenate(finished, axis=0)
    pivots = jnp.sum(jnp.where(lines == lanes, work, 0.0), axis=1, keepdims=True)
    return work[:, k:] * lax.rsqrt(pivots)


def finish_kernel(rows, columns, inverse_count, sums, field, out, projected, staged, sems):
    k = projected.shape[0]
    grid = Grid(rows, columns)
    highest = lax.Precision.HIGHEST
    inverse = inverse_factor(sums[:, :k] * inverse_count)
    parts = split(inverse)
    left = jnp.concatenate([parts, parts], axis=1)
    half = columns // 2

    def copy(row, side):
        piece = pl.ds(side * half, half)
        return pltpu.make_async_copy(
            staged.at[row, :, piece], out.at[:, row, piece], sems.at[2 * row + side]
        )

    def body(step, _):
        row, side = step // 2, step % 2
        for tile in range(0, half, 8):
            first = pl.multiple_of(side * half + tile, 8)
            blocks = []
            for at in range(8):
                both = jnp.dot(left, field[grid.own(row, first + at)], preferred_element_type=F32)
                blocks.append((both[:k] + both[k:])[None])
            staged[row, :, pl.ds(first, 8), :] = pltpu.einshape(
                "dkr->kdr", jnp.concatenate(blocks, axis=0)
            )
        copy(row, side).start()
        return 0

    lax.fori_loop(0, 2 * rows, body, 0)
    moments = sums[:, k:] * inverse_count
    partial = jnp.dot(inverse, moments, precision=highest, preferred_element_type=F32)
    projected[...] = lax.dot_general(
        partial, inverse, (((1,), (1,)), ((), ())), precision=highest, preferred_element_type=F32
    )
    for step in range(2 * rows):
        copy(step // 2, step % 2).wait()


def finish(sums, field, rows, columns, inverse_count):
    k = sums.shape[0]
    width = field.shape[2]
    return pl.pallas_call(
        functools.partial(finish_kernel, rows, columns, inverse_count),
        out_shape=(
            jax.ShapeDtypeStruct((k, rows, columns, width), F32),
            jax.ShapeDtypeStruct((k, k), F32),
        ),
        in_specs=[VMEM, VMEM],
        out_specs=(HBM, VMEM),
        scratch_shapes=[
            pltpu.VMEM((rows, k, columns, width), F32),
            pltpu.SemaphoreType.DMA((2 * rows,)),
        ],
        compiler_params=pltpu.CompilerParams(vmem_limit_bytes=8 << 20),
        name="finish",
    )(sums, placed(field, pltpu.VMEM))


def swap(values, axis, first):
    count = lax.axis_size(axis)
    pairs = []
    for i in range(first, count - 1, 2):
        pairs += [(i, i + 1), (i + 1, i)]
    return lax.ppermute(values, axis, pairs)


def summed(values, axis):
    count = lax.axis_size(axis)
    if count & (count - 1):
        return lax.psum(values, axis)
    bit = 1
    while bit < count:
        values = values + lax.ppermute(values, axis, [(i, i ^ bit) for i in range(count)])
        bit *= 2
    return values


def on_device(start_basis, stiffness, pattern, lumped_mass):
    k, rows, columns, width = start_basis.shape
    flags = jnp.stack([lax.axis_index("sub") % 2, lax.axis_index("dom") % 2]).astype(jnp.int32)
    values = {
        FLAGS: flags,
        STIFFNESS: stiffness,
        START: start_basis,
    }
    made = prepare(flags, start_basis, lumped_mass, jnp.transpose(pattern, (0, 2, 1)))
    values.update(zip((FAR_EDGE, NEAR_EDGE, EVEN, ODD, MASS, PATTERN), made))
    totals = []
    for level in (1, 2, 3):
        values[FAR_HALO] = swap(values[FAR_EDGE], "sub", 1)
        values[NEAR_HALO] = swap(values[NEAR_EDGE], "sub", 0)
        values[EVEN_SIDE] = swap(values[EVEN], "dom", 0)
        values[ODD_SIDE] = swap(values[ODD], "dom", 1)
        values = level_call(level, INNER, values)
        if level < 3:
            far_corner, near_corner = corners(
                values[MARK], values[EVEN_SIDE], values[ODD_SIDE]
            )
            values[FAR_CORNER] = swap(far_corner, "sub", 1)
            values[NEAR_CORNER] = swap(near_corner, "sub", 0)
        values = level_call(level, NEAR, values)
        values = level_call(level, FAR, values)
        if level > 1:
            totals.append(values[TOTAL])
    sums = jnp.concatenate(totals, axis=1)
    for axis in ("sub", "dom"):
        sums = summed(sums, axis)
    vertex_count = rows * columns * width * lax.axis_size("dom") * lax.axis_size("sub")
    return finish(sums, values[OUTER], rows, columns, 1.0 / vertex_count)


def solution(mesh):
    in_specs = (
        P(None, "sub", "dom", None),
        P("sub", "dom", None, None, None),
        P("sub", "dom", None),
        P("sub", "dom", None),
    )
    out_specs = (P(None, "sub", "dom", None), P())
    return jax.shard_map(
        on_device, mesh=mesh, in_specs=in_specs, out_specs=out_specs, check_vma=False
    )
```

```python
import functools

import jax
import jax.numpy as jnp
from jax import lax
from jax.experimental import pallas as pl
from jax.experimental.pallas import tpu as pltpu
from jax.sharding import PartitionSpec as P

F32 = jnp.float32
BF16 = jnp.bfloat16
LONGEST = 32

VMEM = pl.BlockSpec(memory_space=pltpu.VMEM)
SMEM = pl.BlockSpec(memory_space=pltpu.SMEM)
HBM = pl.BlockSpec(memory_space=pltpu.HBM)


(
    FLAGS, PATTERN, MASS, STIFFNESS, LOADED, OUTER, MIDDLE, TOTAL, FAR_EDGE, NEAR_EDGE, EVEN, ODD,
    MARK, START, LOAD_SEMS, EVEN_SIDE, ODD_SIDE, NEAR_HALO, FAR_HALO, FAR_CORNER,
    NEAR_CORNER,
) = range(21)
INNER, NEAR, FAR = range(3)


def split(values):
    head = values.astype(BF16)
    rest = (values - head.astype(F32)).astype(BF16)
    return jnp.concatenate([head, rest], axis=0)


def joined(pair):
    wide = pair.astype(F32)
    half = wide.shape[0] // 2
    return wide[:half] + wide[half:]


def placed(values, space):
    return pltpu.with_memory_space_constraint(values, space)


def dot_last(left, right):
    return lax.dot_general(left, right, (((1,), (1,)), ((), ())), preferred_element_type=F32)


def folded(square):
    half = square.shape[0] // 2
    rows = square[:half] + square[half:]
    return rows[:, :half] + rows[:, half:]


class Grid:
    def __init__(self, rows, columns, flags=None):
        self.rows, self.columns, self.pitch = rows, columns, columns + 2
        self.blocks = (rows + 2) * self.pitch
        if flags is not None:
            lower, left = flags[0], flags[1]
            self.lower, self.left = lower, left
            self.far_row = lower * (rows - 1)
            self.near_row = (1 - lower) * (rows - 1)
            self.far_halo = lower * (rows + 1)
            self.near_halo = (1 - lower) * (rows + 1)
            self.even_col = (1 - left) * (columns - 1)
            self.odd_col = left * (columns - 1)
            self.even_halo = (1 - left) * (columns + 1)
            self.odd_halo = left * (columns + 1)

    def own(self, row, column):
        return (row + 1) * self.pitch + column + 1

    def padded(self, row, column):
        return row * self.pitch + column

    def slot_rows(self):
        return [self.far_row, self.near_row] + list(range(1, self.rows - 1))


def prepare_kernel(
    rows, columns, flags, start, mass, pattern, far, near, even, odd, middle, held_mass,
    held_pattern, staged, sems
):
    grid = Grid(rows, columns, flags)
    order = grid.slot_rows()
    copies = [
        pltpu.make_async_copy(
            start.at[:, order[slot]],
            staged.at[slot] if slot < 2 else middle.at[slot - 2],
            sems.at[slot],
        )
        for slot in range(rows)
    ] + [
        pltpu.make_async_copy(mass, held_mass, sems.at[rows]),
        pltpu.make_async_copy(pattern, held_pattern, sems.at[rows + 1]),
    ]
    for copy in copies:
        copy.start()
    for slot, edge in ((0, far), (1, near)):
        copies[slot].wait()

        def body(step, _):
            first = pl.multiple_of(step * 8, 8)
            tile = pltpu.einshape("kdr->dkr", staged[slot, :, pl.ds(first, 8), :])
            for inner in range(8):
                edge[step * 8 + inner] = tile[inner]
            return 0

        lax.fori_loop(0, columns // 8, body, 0)
        even[slot] = edge[grid.even_col]
        odd[slot] = edge[grid.odd_col]
    even_right = grid.even_col > 0
    for slot in range(2, rows):
        copies[slot].wait()
        first = pltpu.einshape("kdr->dkr", middle[slot - 2, :, :8, :])[0]
        last = pltpu.einshape("kdr->dkr", middle[slot - 2, :, columns - 8 :, :])[7]
        even[slot] = jnp.where(even_right, last, first)
        odd[slot] = jnp.where(even_right, first, last)
    for copy in copies[rows:]:
        copy.wait()


def prepare(flags, start, mass, pattern):
    k, rows, columns, width = start.shape
    edge = jax.ShapeDtypeStruct((columns, k, width), F32)
    side = jax.ShapeDtypeStruct((rows, k, width), F32)
    return pl.pallas_call(
        functools.partial(prepare_kernel, rows, columns),
        out_shape=(
            edge,
            edge,
            side,
            side,
            pltpu.VMEM((rows - 2, k, columns, width), F32),
            pltpu.VMEM(mass.shape, F32),
            pltpu.VMEM(pattern.shape, jnp.int32),
        ),
        in_specs=[SMEM, HBM, HBM, HBM],
        out_specs=(VMEM,) * 7,
        scratch_shapes=[
            pltpu.VMEM((2, k, columns, width), F32),
            pltpu.SemaphoreType.DMA((rows + 2,)),
        ],
        compiler_params=pltpu.CompilerParams(vmem_limit_bytes=4 << 20),
        name="prepare",
    )(flags, *(placed(values, pltpu.HBM) for values in (start, mass, pattern)))


def corners_kernel(mark, even_side, odd_side, far_corner, near_corner):
    for slot, corner in enumerate((far_corner, near_corner)):
        corner[0] = even_side[slot]
        corner[1] = odd_side[slot]


def corners(mark, even_side, odd_side):
    shape = jax.ShapeDtypeStruct((2,) + even_side.shape[1:], F32)
    return pl.pallas_call(
        corners_kernel,
        out_shape=(shape, shape),
        in_specs=[SMEM, VMEM, VMEM],
        out_specs=(VMEM, VMEM),
        compiler_params=pltpu.CompilerParams(vmem_limit_bytes=1 << 20),
        name="corners",
    )(mark, even_side, odd_side)


def stride_of(count):
    return max(size for size in range(1, LONGEST + 1) if count % size == 0)


def level_kernel(level, part, rows, columns, ref):
    grid = Grid(rows, columns, ref[FLAGS])
    pattern, mass = ref[PATTERN], ref[MASS]
    total = ref.get(TOTAL)
    base = ref[OUTER]
    field = ref[MIDDLE] if level == 2 else ref[OUTER]
    result = {1: ref.get(MIDDLE), 2: ref[OUTER], 3: None}[level]
    stiffness = ref[LOADED] if LOADED in ref else ref[STIFFNESS]
    order = grid.slot_rows()

    loads, ahead = 0, 3
    if LOADED in ref:
        half = columns // 2

        def load(at):
            row = grid.far_row
            if part == INNER:
                row = jnp.where(at // 2 < rows - 2, 1 + at // 2, grid.near_row)
            piece = (row, pl.ds(at % 2 * half, half))
            return pltpu.make_async_copy(
                ref[STIFFNESS].at[piece], ref[LOADED].at[piece], ref[LOAD_SEMS].at[at]
            )

        loads = 2 * rows - 2 if part == INNER else 2
    for at in range(ahead if part == INNER and loads else loads):
        load(at).start()

    def fill(row, blocks):
        def body(step, _):
            for inner in range(8):
                column = step * 8 + inner
                field[grid.padded(row, column + 1)] = split(blocks[column])
            return 0

        lax.fori_loop(0, columns // 8, body, 0)

    if level == 1 and part == INNER:
        fill(grid.far_row + 1, ref[FAR_EDGE])
        fill(grid.near_row + 1, ref[NEAR_EDGE])
        for slot in range(2, rows):

            def relay(step, _):
                first = pl.multiple_of(step * 8, 8)
                values = ref[START][slot - 2, :, pl.ds(first, 8), :]
                tile = pltpu.einshape("kdr->dkr", values)
                for inner in range(8):
                    field[grid.own(order[slot], step * 8 + inner)] = split(tile[inner])
                return 0

            lax.fori_loop(0, columns // 8, relay, 0)
    if part == NEAR:
        for slot, row in enumerate(order):
            field[grid.padded(row + 1, grid.even_halo)] = split(ref[EVEN_SIDE][slot])
            field[grid.padded(row + 1, grid.odd_halo)] = split(ref[ODD_SIDE][slot])
        fill(grid.near_halo, ref[NEAR_HALO])
    if part == FAR:
        for row, name in ((grid.far_halo, FAR_CORNER), (grid.near_halo, NEAR_CORNER)):
            for at, halo in enumerate((grid.even_halo, grid.odd_halo)):
                if level == 3:
                    field[grid.padded(row, halo)] = jnp.zeros(field.shape[1:], BF16)
                else:
                    field[grid.padded(row, halo)] = split(ref[name][at])
        fill(grid.far_halo, ref[FAR_HALO])

    def block(row, column, edge):
        corner = grid.padded(row, column)
        own = grid.own(row, column)
        blocks = [field[own]]
        for slot in range(1, 4):
            offset = pattern[row, slot, column]
            blocks.append(field[corner + offset + (grid.pitch - 3) * ((offset * 11) >> 5)])
        matrix = jnp.concatenate([stiffness[row, column, slot] for slot in range(4)], axis=1)
        products = dot_last(jnp.concatenate(blocks, axis=1), matrix)
        half = products.shape[0] // 2
        coupled = products[:half] + products[half:]
        if level == 3:
            return blocks[0], split(coupled)
        weight = mass[row, pl.ds(column, 1), :]
        scaled = coupled * (1.0 / (3.0 * weight)) - (4.0 / 3.0) * joined(blocks[0])
        if level == 2:
            scaled = 2.0 * scaled - joined(base[own])
        pair = split(scaled)
        result[own] = pair
        if edge is not None:
            edge[column] = scaled
        return (split(scaled * weight), pair) if level == 2 else (None, None)

    def add_terms(terms):
        if level == 1:
            return
        sums = None
        for at in range(0, len(terms), 4):
            lefts, rights = zip(*terms[at : at + 4])
            term = dot_last(jnp.concatenate(lefts, axis=1), jnp.concatenate(rights, axis=1))
            sums = term if sums is None else sums + term
        total[...] += folded(sums)

    def sweep(row, first, count, edge):
        size = stride_of(count)

        def body(step, _):
            add_terms([block(row, first + step * size + at, edge) for at in range(size)])
            return 0

        lax.fori_loop(0, count // size, body, 0)

    near_edge = ref.get(NEAR_EDGE) if level < 3 else None
    if part == INNER:
        ref[MARK][0] = 0
        if level > 1:
            total[...] = jnp.zeros_like(total)
        size = (columns - 2) // 2 if level == 1 else stride_of(columns - 2)
        groups = (columns - 2) // size

        def body(step, _):
            row = 1 + step // groups
            first = 1 + (step % groups) * size
            if loads:
                load(step).wait()

                @pl.when(step + ahead < loads)
                def _():
                    load(step + ahead).start()

            add_terms([block(row, first + at, None) for at in range(size)])
            return 0

        lax.fori_loop(0, (rows - 2) * groups, body, 0)
        if loads:
            for at in range(2 * rows - 4 + ahead, loads):
                load(at).start()
            for at in range(2 * rows - 4, loads):
                load(at).wait()
    ends = (0, columns - 1)
    if part == NEAR:
        sweep(grid.near_row, 1, columns - 2, near_edge)
        add_terms([block(row, column, None) for row in order[2:] for column in ends])
        for at in range(loads):
            load(at).wait()
    if part == FAR:
        sweep(grid.far_row, 0, columns, ref.get(FAR_EDGE) if level < 3 else None)
        add_terms([block(grid.near_row, column, near_edge) for column in ends])
    if level == 3 and part != INNER:
        slot = rows + (part == NEAR)
        halo = ref[NEAR_HALO] if part == NEAR else ref[FAR_HALO]
        for name, column in ((EVEN_SIDE, grid.even_col), (ODD_SIDE, grid.odd_col)):
            total[...] += folded(dot_last(split(ref[name][slot]), split(halo[column])))
    if level == 2 and part == FAR:
        for slot, row in enumerate(order[:2]):
            down = grid.lower * 2 - 1 if slot == 0 else 1 - grid.lower * 2
            for name, column, right in (
                (EVEN, grid.even_col, 1 - grid.left * 2),
                (ODD, grid.odd_col, grid.left * 2 - 1),
            ):
                across = 3 * (down + 1) + right + 1
                matrix = jnp.zeros(stiffness.shape[3:], BF16)
                for at in range(1, 4):
                    hit = pattern[row, at, column] == across
                    matrix = jnp.where(hit, stiffness[row, column, at], matrix)
                values = jnp.dot(
                    result[grid.own(row, column)], matrix, preferred_element_type=F32
                )
                half = values.shape[0] // 2
                ref[name][rows + slot] = values[:half] + values[half:]
    if level < 3 and part != INNER:
        for slot, row in enumerate(order):
            if (slot < 2) == (part == FAR):
                ref[EVEN][slot] = joined(result[grid.own(row, grid.even_col)])
                ref[ODD][slot] = joined(result[grid.own(row, grid.odd_col)])


def level_call(level, part, values):
    columns, k, width = values[NEAR_EDGE].shape
    rows = values[MASS].shape[0]
    grid = Grid(rows, columns)
    edge = jax.ShapeDtypeStruct((columns, k, width), F32)
    side = jax.ShapeDtypeStruct((rows + 2 * (level == 2), k, width), F32)
    pair = pltpu.VMEM((grid.blocks, 2 * k, width), BF16)
    shapes = {
        OUTER: pair,
        MIDDLE: pair,
        FAR_EDGE: edge,
        NEAR_EDGE: edge,
        EVEN: side,
        ODD: side,
        MARK: jax.ShapeDtypeStruct((1,), jnp.int32),
        TOTAL: jax.ShapeDtypeStruct((k, k), F32),
        LOADED: pltpu.VMEM(values[STIFFNESS].shape, BF16),
    }
    read = [FLAGS, PATTERN, MASS]
    updated, made = [], []
    if level == 1 and part != FAR:
        read.append(STIFFNESS)
        (made if part == INNER else updated).append(LOADED)
    else:
        read.append(LOADED)
    (made if (level, part) == (1, INNER) else updated).extend(
        [OUTER, MIDDLE] if level < 3 else [OUTER]
    )
    if level > 1:
        (made if part == INNER else updated).append(TOTAL)
    scratch = {}
    if part == INNER:
        made.append(MARK)
        if level == 1:
            read += [START, FAR_EDGE, NEAR_EDGE]
            scratch[LOAD_SEMS] = pltpu.SemaphoreType.DMA((2 * rows - 2,))
    elif part == NEAR:
        read += [EVEN_SIDE, ODD_SIDE, NEAR_HALO]
        made += [NEAR_EDGE, EVEN, ODD] if level < 3 else []
        if level == 1:
            scratch[LOAD_SEMS] = pltpu.SemaphoreType.DMA((2,))
    else:
        read.append(FAR_HALO)
        read += [FAR_CORNER, NEAR_CORNER] if level < 3 else [EVEN_SIDE, ODD_SIDE]
        updated += [NEAR_EDGE, EVEN, ODD] if level < 3 else []
        made += [FAR_EDGE] if level < 3 else []
    specs = {FLAGS: SMEM, PATTERN: SMEM, MARK: SMEM, STIFFNESS: HBM}
    spaces = dict.fromkeys((OUTER, MIDDLE, LOADED, MASS, PATTERN, START), pltpu.VMEM)
    spaces.update({STIFFNESS: pltpu.HBM})

    def kernel(*refs):
        skipped = len(read) + len(updated)
        names = read + updated + made + list(scratch)
        ref = dict(zip(names, refs[: len(read)] + refs[skipped:]))
        if LOADED in read:
            ref[STIFFNESS] = ref.pop(LOADED)
        level_kernel(level, part, rows, columns, ref)

    outs = pl.pallas_call(
        kernel,
        out_shape=tuple(shapes[name] for name in updated + made),
        in_specs=[specs.get(name, VMEM) for name in read + updated],
        out_specs=tuple(specs.get(name, VMEM) for name in updated + made),
        scratch_shapes=list(scratch.values()),
        input_output_aliases={len(read) + at: at for at in range(len(updated))},
        compiler_params=pltpu.CompilerParams(vmem_limit_bytes=6 << 20),
        name=("inner", "near", "far")[part],
    )(*[placed(values[name], spaces[name]) if name in spaces else values[name]
        for name in read + updated])
    return {**values, **dict(zip(updated + made, outs))}


def inverse_factor(gram):
    k, step = gram.shape[0], 8
    lines = lax.broadcasted_iota(jnp.int32, (k, 2 * k), 0)
    lanes = lax.broadcasted_iota(jnp.int32, (k, 2 * k), 1)
    work = jnp.concatenate([gram, (lines == lanes).astype(F32)[:, :k]], axis=1)
    finished = []
    for first in range(0, k, step):
        rows = [work[at : at + 1] for at in range(step)]
        columns = [
            jnp.broadcast_to(work[:, first + at : first + at + 1], work.shape)
            for at in range(step)
        ]
        entries = [
            [jnp.broadcast_to(rows[i][:, first + j : first + j + 1], (1, 2 * k)) for j in range(step)]
            for i in range(step)
        ]
        change = None
        for i in range(step):
            scale = 1.0 / entries[i][i]
            line = rows[i] * scale
            for j in range(i + 1, step):
                factor = entries[i][j] * scale
                for t in range(j, step):
                    entries[j][t] = entries[j][t] - factor * entries[i][t]
                rows[j] = rows[j] - factor * rows[i]
                columns[j] = columns[j] - columns[i] * factor
            column = jnp.where(lines[:step] > i, columns[i][:step], 0.0)
            if work.shape[0] > step:
                column = jnp.concatenate([column, columns[i][step:]], axis=0)
            change = column * line if change is None else change + column * line
        work = work - change
        finished.append(work[:step])
        work = work[step:]
    work = jnp.concatenate(finished, axis=0)
    pivots = jnp.sum(jnp.where(lines == lanes, work, 0.0), axis=1, keepdims=True)
    return work[:, k:] * lax.rsqrt(pivots)


def finish_kernel(rows, columns, inverse_count, sums, field, out, projected, staged, sems):
    k = projected.shape[0]
    grid = Grid(rows, columns)
    highest = lax.Precision.HIGHEST
    inverse = inverse_factor(sums[:, :k] * inverse_count)
    parts = split(inverse)
    left = jnp.concatenate([parts, parts], axis=1)
    half = columns // 2

    def copy(row, side):
        piece = pl.ds(side * half, half)
        return pltpu.make_async_copy(
            staged.at[row, :, piece], out.at[:, row, piece], sems.at[2 * row + side]
        )

    def body(step, _):
        row, side = step // 2, step % 2
        for tile in range(0, half, 8):
            first = pl.multiple_of(side * half + tile, 8)
            blocks = []
            for at in range(8):
                both = jnp.dot(left, field[grid.own(row, first + at)], preferred_element_type=F32)
                blocks.append((both[:k] + both[k:])[None])
            staged[row, :, pl.ds(first, 8), :] = pltpu.einshape(
                "dkr->kdr", jnp.concatenate(blocks, axis=0)
            )
        copy(row, side).start()
        return 0

    lax.fori_loop(0, 2 * rows, body, 0)
    moments = sums[:, k:] * inverse_count
    partial = jnp.dot(inverse, moments, precision=highest, preferred_element_type=F32)
    projected[...] = lax.dot_general(
        partial, inverse, (((1,), (1,)), ((), ())), precision=highest, preferred_element_type=F32
    )
    for step in range(2 * rows):
        copy(step // 2, step % 2).wait()


def finish(sums, field, rows, columns, inverse_count):
    k = sums.shape[0]
    width = field.shape[2]
    return pl.pallas_call(
        functools.partial(finish_kernel, rows, columns, inverse_count),
        out_shape=(
            jax.ShapeDtypeStruct((k, rows, columns, width), F32),
            jax.ShapeDtypeStruct((k, k), F32),
        ),
        in_specs=[VMEM, VMEM],
        out_specs=(HBM, VMEM),
        scratch_shapes=[
            pltpu.VMEM((rows, k, columns, width), F32),
            pltpu.SemaphoreType.DMA((2 * rows,)),
        ],
        compiler_params=pltpu.CompilerParams(vmem_limit_bytes=8 << 20),
        name="finish",
    )(sums, placed(field, pltpu.VMEM))


def swap(values, axis, first):
    count = lax.axis_size(axis)
    pairs = []
    for i in range(first, count - 1, 2):
        pairs += [(i, i + 1), (i + 1, i)]
    return lax.ppermute(values, axis, pairs)


def summed(values, axis):
    count = lax.axis_size(axis)
    if count & (count - 1):
        return lax.psum(values, axis)
    bit = 1
    while bit < count:
        values = values + lax.ppermute(values, axis, [(i, i ^ bit) for i in range(count)])
        bit *= 2
    return values


def on_device(start_basis, stiffness, pattern, lumped_mass):
    k, rows, columns, width = start_basis.shape
    flags = jnp.stack([lax.axis_index("sub") % 2, lax.axis_index("dom") % 2]).astype(jnp.int32)
    values = {
        FLAGS: flags,
        STIFFNESS: stiffness,
    }
    made = prepare(flags, start_basis, lumped_mass, jnp.transpose(pattern, (0, 2, 1)))
    values.update(zip((FAR_EDGE, NEAR_EDGE, EVEN, ODD, START, MASS, PATTERN), made))
    totals = []
    for level in (1, 2, 3):
        values[FAR_HALO] = swap(values[FAR_EDGE], "sub", 1)
        values[NEAR_HALO] = swap(values[NEAR_EDGE], "sub", 0)
        values[EVEN_SIDE] = swap(values[EVEN], "dom", 0)
        values[ODD_SIDE] = swap(values[ODD], "dom", 1)
        values = level_call(level, INNER, values)
        if level < 3:
            far_corner, near_corner = corners(
                values[MARK], values[EVEN_SIDE], values[ODD_SIDE]
            )
            values[FAR_CORNER] = swap(far_corner, "sub", 1)
            values[NEAR_CORNER] = swap(near_corner, "sub", 0)
        values = level_call(level, NEAR, values)
        values = level_call(level, FAR, values)
        if level > 1:
            totals.append(values[TOTAL])
    sums = jnp.concatenate(totals, axis=1)
    for axis in ("sub", "dom"):
        sums = summed(sums, axis)
    vertex_count = rows * columns * width * lax.axis_size("dom") * lax.axis_size("sub")
    return finish(sums, values[OUTER], rows, columns, 1.0 / vertex_count)


def solution(mesh):
    in_specs = (
        P(None, "sub", "dom", None),
        P("sub", "dom", None, None, None),
        P("sub", "dom", None),
        P("sub", "dom", None),
    )
    out_specs = (P(None, "sub", "dom", None), P())
    return jax.shard_map(
        on_device, mesh=mesh, in_specs=in_specs, out_specs=out_specs, check_vma=False
    )
```

```python
import functools

import jax
import jax.numpy as jnp
from jax import lax
from jax.experimental import pallas as pl
from jax.experimental.pallas import tpu as pltpu
from jax.sharding import PartitionSpec as P

F32 = jnp.float32
BF16 = jnp.bfloat16
LONGEST = 32

VMEM = pl.BlockSpec(memory_space=pltpu.VMEM)
SMEM = pl.BlockSpec(memory_space=pltpu.SMEM)
HBM = pl.BlockSpec(memory_space=pltpu.HBM)


(
    FLAGS, PATTERN, MASS, STIFFNESS, LOADED, OUTER, MIDDLE, TOTAL, FAR_EDGE, NEAR_EDGE, EVEN, ODD,
    MARK, START, LOAD_SEMS, EVEN_SIDE, ODD_SIDE, NEAR_HALO, FAR_HALO, FAR_CORNER,
    NEAR_CORNER,
) = range(21)
INNER, NEAR, FAR = range(3)


def split(values):
    head = values.astype(BF16)
    rest = (values - head.astype(F32)).astype(BF16)
    return jnp.concatenate([head, rest], axis=0)


def joined(pair):
    wide = pair.astype(F32)
    half = wide.shape[0] // 2
    return wide[:half] + wide[half:]


def placed(values, space):
    return pltpu.with_memory_space_constraint(values, space)


def dot_last(left, right):
    return lax.dot_general(left, right, (((1,), (1,)), ((), ())), preferred_element_type=F32)


def folded(square):
    half = square.shape[0] // 2
    rows = square[:half] + square[half:]
    return rows[:, :half] + rows[:, half:]


class Grid:
    def __init__(self, rows, columns, flags=None):
        self.rows, self.columns, self.pitch = rows, columns, columns + 2
        self.blocks = (rows + 2) * self.pitch
        if flags is not None:
            lower, left = flags[0], flags[1]
            self.lower, self.left = lower, left
            self.far_row = lower * (rows - 1)
            self.near_row = (1 - lower) * (rows - 1)
            self.far_halo = lower * (rows + 1)
            self.near_halo = (1 - lower) * (rows + 1)
            self.even_col = (1 - left) * (columns - 1)
            self.odd_col = left * (columns - 1)
            self.even_halo = (1 - left) * (columns + 1)
            self.odd_halo = left * (columns + 1)

    def own(self, row, column):
        return (row + 1) * self.pitch + column + 1

    def padded(self, row, column):
        return row * self.pitch + column

    def slot_rows(self):
        return [self.far_row, self.near_row] + list(range(1, self.rows - 1))


def prepare_kernel(
    rows, columns, flags, start, mass, pattern, far, near, even, odd, middle, held_mass,
    held_pattern, field, staged, sems
):
    grid = Grid(rows, columns, flags)
    order = grid.slot_rows()
    copies = [
        pltpu.make_async_copy(
            start.at[:, order[slot]],
            staged.at[slot] if slot < 2 else middle.at[slot - 2],
            sems.at[slot],
        )
        for slot in range(rows)
    ] + [
        pltpu.make_async_copy(mass, held_mass, sems.at[rows]),
        pltpu.make_async_copy(pattern, held_pattern, sems.at[rows + 1]),
    ]
    for copy in copies:
        copy.start()
    for slot, edge in ((0, far), (1, near)):
        copies[slot].wait()

        def body(step, _):
            first = pl.multiple_of(step * 8, 8)
            tile = pltpu.einshape("kdr->dkr", staged[slot, :, pl.ds(first, 8), :])
            for inner in range(8):
                edge[step * 8 + inner] = tile[inner]
                field[grid.own(order[slot], step * 8 + inner)] = split(tile[inner])
            return 0

        lax.fori_loop(0, columns // 8, body, 0)
        even[slot] = edge[grid.even_col]
        odd[slot] = edge[grid.odd_col]
    even_right = grid.even_col > 0
    for slot in range(2, rows):
        copies[slot].wait()
        first = pltpu.einshape("kdr->dkr", middle[slot - 2, :, :8, :])[0]
        last = pltpu.einshape("kdr->dkr", middle[slot - 2, :, columns - 8 :, :])[7]
        even[slot] = jnp.where(even_right, last, first)
        odd[slot] = jnp.where(even_right, first, last)
    for copy in copies[rows:]:
        copy.wait()


def prepare(flags, start, mass, pattern):
    k, rows, columns, width = start.shape
    edge = jax.ShapeDtypeStruct((columns, k, width), F32)
    side = jax.ShapeDtypeStruct((rows, k, width), F32)
    return pl.pallas_call(
        functools.partial(prepare_kernel, rows, columns),
        out_shape=(
            edge,
            edge,
            side,
            side,
            pltpu.VMEM((rows - 2, k, columns, width), F32),
            pltpu.VMEM(mass.shape, F32),
            pltpu.VMEM(pattern.shape, jnp.int32),
            pltpu.VMEM((Grid(rows, columns).blocks, 2 * k, width), BF16),
        ),
        in_specs=[SMEM, HBM, HBM, HBM],
        out_specs=(VMEM,) * 8,
        scratch_shapes=[
            pltpu.VMEM((2, k, columns, width), F32),
            pltpu.SemaphoreType.DMA((rows + 2,)),
        ],
        compiler_params=pltpu.CompilerParams(vmem_limit_bytes=4 << 20),
        name="prepare",
    )(flags, *(placed(values, pltpu.HBM) for values in (start, mass, pattern)))


def corners_kernel(mark, even_side, odd_side, far_corner, near_corner):
    for slot, corner in enumerate((far_corner, near_corner)):
        corner[0] = even_side[slot]
        corner[1] = odd_side[slot]


def corners(mark, even_side, odd_side):
    shape = jax.ShapeDtypeStruct((2,) + even_side.shape[1:], F32)
    return pl.pallas_call(
        corners_kernel,
        out_shape=(shape, shape),
        in_specs=[SMEM, VMEM, VMEM],
        out_specs=(VMEM, VMEM),
        compiler_params=pltpu.CompilerParams(vmem_limit_bytes=1 << 20),
        name="corners",
    )(mark, even_side, odd_side)


def stride_of(count):
    return max(size for size in range(1, LONGEST + 1) if count % size == 0)


def level_kernel(level, part, rows, columns, ref):
    grid = Grid(rows, columns, ref[FLAGS])
    pattern, mass = ref[PATTERN], ref[MASS]
    total = ref.get(TOTAL)
    base = ref[OUTER]
    field = ref[MIDDLE] if level == 2 else ref[OUTER]
    result = {1: ref.get(MIDDLE), 2: ref[OUTER], 3: None}[level]
    stiffness = ref[LOADED] if LOADED in ref else ref[STIFFNESS]
    order = grid.slot_rows()

    loads, ahead = 0, 3
    if LOADED in ref:
        half = columns // 2

        def load(at):
            row = grid.far_row
            if part == INNER:
                row = jnp.where(at // 2 < rows - 2, 1 + at // 2, grid.near_row)
            piece = (row, pl.ds(at % 2 * half, half))
            return pltpu.make_async_copy(
                ref[STIFFNESS].at[piece], ref[LOADED].at[piece], ref[LOAD_SEMS].at[at]
            )

        loads = 2 * rows - 2 if part == INNER else 2
    for at in range(ahead if part == INNER and loads else loads):
        load(at).start()

    def fill(row, blocks):
        def body(step, _):
            for inner in range(16):
                column = step * 16 + inner
                field[grid.padded(row, column + 1)] = split(blocks[column])
            return 0

        lax.fori_loop(0, columns // 16, body, 0)

    if level == 1 and part == INNER:
        for slot in range(2, rows):

            def relay(step, _):
                first = pl.multiple_of(step * 8, 8)
                values = ref[START][slot - 2, :, pl.ds(first, 8), :]
                tile = pltpu.einshape("kdr->dkr", values)
                for inner in range(8):
                    field[grid.own(order[slot], step * 8 + inner)] = split(tile[inner])
                return 0

            lax.fori_loop(0, columns // 8, relay, 0)
    if part == NEAR:
        for slot, row in enumerate(order):
            field[grid.padded(row + 1, grid.even_halo)] = split(ref[EVEN_SIDE][slot])
            field[grid.padded(row + 1, grid.odd_halo)] = split(ref[ODD_SIDE][slot])
        fill(grid.near_halo, ref[NEAR_HALO])
    if part == FAR:
        for row, name in ((grid.far_halo, FAR_CORNER), (grid.near_halo, NEAR_CORNER)):
            for at, halo in enumerate((grid.even_halo, grid.odd_halo)):
                if level == 3:
                    field[grid.padded(row, halo)] = jnp.zeros(field.shape[1:], BF16)
                else:
                    field[grid.padded(row, halo)] = split(ref[name][at])
        fill(grid.far_halo, ref[FAR_HALO])

    def block(row, column, edge):
        corner = grid.padded(row, column)
        own = grid.own(row, column)
        blocks = [field[own]]
        for slot in range(1, 4):
            offset = pattern[row, slot, column]
            blocks.append(field[corner + offset + (grid.pitch - 3) * ((offset * 11) >> 5)])
        matrix = jnp.concatenate([stiffness[row, column, slot] for slot in range(4)], axis=1)
        products = dot_last(jnp.concatenate(blocks, axis=1), matrix)
        half = products.shape[0] // 2
        coupled = products[:half] + products[half:]
        if level == 3:
            return blocks[0], split(coupled)
        weight = mass[row, pl.ds(column, 1), :]
        scaled = coupled * (1.0 / (3.0 * weight)) - (4.0 / 3.0) * joined(blocks[0])
        if level == 2:
            scaled = 2.0 * scaled - joined(base[own])
        pair = split(scaled)
        result[own] = pair
        if edge is not None:
            edge[column] = scaled
        return (split(scaled * weight), pair) if level == 2 else (None, None)

    def add_terms(terms):
        if level == 1:
            return
        sums = None
        for at in range(0, len(terms), 8):
            lefts, rights = zip(*terms[at : at + 8])
            term = dot_last(jnp.concatenate(lefts, axis=1), jnp.concatenate(rights, axis=1))
            sums = term if sums is None else sums + term
        total[...] += folded(sums)

    def sweep(row, first, count, edge):
        size = stride_of(count)

        def body(step, _):
            add_terms([block(row, first + step * size + at, edge) for at in range(size)])
            return 0

        lax.fori_loop(0, count // size, body, 0)

    near_edge = ref.get(NEAR_EDGE) if level < 3 else None
    if part == INNER:
        ref[MARK][0] = 0
        if level > 1:
            total[...] = jnp.zeros_like(total)
        size = (columns - 2) // 2 if level == 1 else stride_of(columns - 2)
        groups = (columns - 2) // size

        def body(step, _):
            row = 1 + step // groups
            first = 1 + (step % groups) * size
            if loads:
                load(step).wait()

                @pl.when(step + ahead < loads)
                def _():
                    load(step + ahead).start()

            add_terms([block(row, first + at, None) for at in range(size)])
            return 0

        lax.fori_loop(0, (rows - 2) * groups, body, 0)
        if loads:
            for at in range(2 * rows - 4 + ahead, loads):
                load(at).start()
            for at in range(2 * rows - 4, loads):
                load(at).wait()
    ends = (0, columns - 1)
    if part == NEAR:
        sweep(grid.near_row, 1, columns - 2, near_edge)
        add_terms([block(row, column, None) for row in order[2:] for column in ends])
        for at in range(loads):
            load(at).wait()
    if part == FAR:
        sweep(grid.far_row, 0, columns, ref.get(FAR_EDGE) if level < 3 else None)
        add_terms([block(grid.near_row, column, near_edge) for column in ends])
    if level == 3 and part != INNER:
        slot = rows + (part == NEAR)
        halo = ref[NEAR_HALO] if part == NEAR else ref[FAR_HALO]
        for name, column in ((EVEN_SIDE, grid.even_col), (ODD_SIDE, grid.odd_col)):
            total[...] += folded(dot_last(split(ref[name][slot]), split(halo[column])))
    if level == 2 and part == FAR:
        for slot, row in enumerate(order[:2]):
            down = grid.lower * 2 - 1 if slot == 0 else 1 - grid.lower * 2
            for name, column, right in (
                (EVEN, grid.even_col, 1 - grid.left * 2),
                (ODD, grid.odd_col, grid.left * 2 - 1),
            ):
                across = 3 * (down + 1) + right + 1
                matrix = jnp.zeros(stiffness.shape[3:], BF16)
                for at in range(1, 4):
                    hit = pattern[row, at, column] == across
                    matrix = jnp.where(hit, stiffness[row, column, at], matrix)
                values = jnp.dot(
                    result[grid.own(row, column)], matrix, preferred_element_type=F32
                )
                half = values.shape[0] // 2
                ref[name][rows + slot] = values[:half] + values[half:]
    if level < 3 and part != INNER:
        for slot, row in enumerate(order):
            if (slot < 2) == (part == FAR):
                ref[EVEN][slot] = joined(result[grid.own(row, grid.even_col)])
                ref[ODD][slot] = joined(result[grid.own(row, grid.odd_col)])


def level_call(level, part, values):
    columns, k, width = values[NEAR_EDGE].shape
    rows = values[MASS].shape[0]
    grid = Grid(rows, columns)
    edge = jax.ShapeDtypeStruct((columns, k, width), F32)
    side = jax.ShapeDtypeStruct((rows + 2 * (level == 2), k, width), F32)
    pair = pltpu.VMEM((grid.blocks, 2 * k, width), BF16)
    shapes = {
        OUTER: pair,
        MIDDLE: pair,
        FAR_EDGE: edge,
        NEAR_EDGE: edge,
        EVEN: side,
        ODD: side,
        MARK: jax.ShapeDtypeStruct((1,), jnp.int32),
        TOTAL: jax.ShapeDtypeStruct((k, k), F32),
        LOADED: pltpu.VMEM(values[STIFFNESS].shape, BF16),
    }
    read = [FLAGS, PATTERN, MASS]
    updated, made = [], []
    if level == 1 and part != FAR:
        read.append(STIFFNESS)
        (made if part == INNER else updated).append(LOADED)
    else:
        read.append(LOADED)
    updated.append(OUTER)
    if level < 3:
        (made if (level, part) == (1, INNER) else updated).append(MIDDLE)
    if level > 1:
        (made if part == INNER else updated).append(TOTAL)
    scratch = {}
    if part == INNER:
        made.append(MARK)
        if level == 1:
            read.append(START)
            scratch[LOAD_SEMS] = pltpu.SemaphoreType.DMA((2 * rows - 2,))
    elif part == NEAR:
        read += [EVEN_SIDE, ODD_SIDE, NEAR_HALO]
        made += [NEAR_EDGE, EVEN, ODD] if level < 3 else []
        if level == 1:
            scratch[LOAD_SEMS] = pltpu.SemaphoreType.DMA((2,))
    else:
        read.append(FAR_HALO)
        read += [FAR_CORNER, NEAR_CORNER] if level < 3 else [EVEN_SIDE, ODD_SIDE]
        updated += [NEAR_EDGE, EVEN, ODD] if level < 3 else []
        made += [FAR_EDGE] if level < 3 else []
    specs = {FLAGS: SMEM, PATTERN: SMEM, MARK: SMEM, STIFFNESS: HBM}
    spaces = dict.fromkeys((OUTER, MIDDLE, LOADED, MASS, PATTERN, START), pltpu.VMEM)
    spaces.update({STIFFNESS: pltpu.HBM})

    def kernel(*refs):
        skipped = len(read) + len(updated)
        names = read + updated + made + list(scratch)
        ref = dict(zip(names, refs[: len(read)] + refs[skipped:]))
        if LOADED in read:
            ref[STIFFNESS] = ref.pop(LOADED)
        level_kernel(level, part, rows, columns, ref)

    outs = pl.pallas_call(
        kernel,
        out_shape=tuple(shapes[name] for name in updated + made),
        in_specs=[specs.get(name, VMEM) for name in read + updated],
        out_specs=tuple(specs.get(name, VMEM) for name in updated + made),
        scratch_shapes=list(scratch.values()),
        input_output_aliases={len(read) + at: at for at in range(len(updated))},
        compiler_params=pltpu.CompilerParams(vmem_limit_bytes=6 << 20),
        name=("inner", "near", "far")[part],
    )(*[placed(values[name], spaces[name]) if name in spaces else values[name]
        for name in read + updated])
    return {**values, **dict(zip(updated + made, outs))}


def inverse_factor(gram):
    k, step = gram.shape[0], 8
    lines = lax.broadcasted_iota(jnp.int32, (k, 2 * k), 0)
    lanes = lax.broadcasted_iota(jnp.int32, (k, 2 * k), 1)
    work = jnp.concatenate([gram, (lines == lanes).astype(F32)[:, :k]], axis=1)
    finished = []
    for first in range(0, k, step):
        rows = [work[at : at + 1] for at in range(step)]
        columns = [
            jnp.broadcast_to(work[:, first + at : first + at + 1], work.shape)
            for at in range(step)
        ]
        entries = [
            [jnp.broadcast_to(rows[i][:, first + j : first + j + 1], (1, 2 * k)) for j in range(step)]
            for i in range(step)
        ]
        change = None
        for i in range(step):
            scale = 1.0 / entries[i][i]
            line = rows[i] * scale
            for j in range(i + 1, step):
                factor = entries[i][j] * scale
                for t in range(j, step):
                    entries[j][t] = entries[j][t] - factor * entries[i][t]
                rows[j] = rows[j] - factor * rows[i]
                columns[j] = columns[j] - columns[i] * factor
            column = jnp.where(lines[:step] > i, columns[i][:step], 0.0)
            if work.shape[0] > step:
                column = jnp.concatenate([column, columns[i][step:]], axis=0)
            change = column * line if change is None else change + column * line
        work = work - change
        finished.append(work[:step])
        work = work[step:]
    work = jnp.concatenate(finished, axis=0)
    pivots = jnp.sum(jnp.where(lines == lanes, work, 0.0), axis=1, keepdims=True)
    return work[:, k:] * lax.rsqrt(pivots)


def finish_kernel(rows, columns, inverse_count, sums, field, out, projected, staged, sems):
    k = projected.shape[0]
    grid = Grid(rows, columns)
    highest = lax.Precision.HIGHEST
    inverse = inverse_factor(sums[:, :k] * inverse_count)
    parts = split(inverse)
    left = jnp.concatenate([parts, parts], axis=1)
    half = columns // 2

    def copy(row, side):
        piece = pl.ds(side * half, half)
        return pltpu.make_async_copy(
            staged.at[row, :, piece], out.at[:, row, piece], sems.at[2 * row + side]
        )

    def body(step, _):
        row, side = step // 2, step % 2
        for tile in range(0, half, 8):
            first = pl.multiple_of(side * half + tile, 8)
            blocks = []
            for at in range(8):
                both = jnp.dot(left, field[grid.own(row, first + at)], preferred_element_type=F32)
                blocks.append((both[:k] + both[k:])[None])
            staged[row, :, pl.ds(first, 8), :] = pltpu.einshape(
                "dkr->kdr", jnp.concatenate(blocks, axis=0)
            )
        copy(row, side).start()
        return 0

    lax.fori_loop(0, 2 * rows, body, 0)
    moments = sums[:, k:] * inverse_count
    partial = jnp.dot(inverse, moments, precision=highest, preferred_element_type=F32)
    projected[...] = lax.dot_general(
        partial, inverse, (((1,), (1,)), ((), ())), precision=highest, preferred_element_type=F32
    )
    for step in range(2 * rows):
        copy(step // 2, step % 2).wait()


def finish(sums, field, rows, columns, inverse_count):
    k = sums.shape[0]
    width = field.shape[2]
    return pl.pallas_call(
        functools.partial(finish_kernel, rows, columns, inverse_count),
        out_shape=(
            jax.ShapeDtypeStruct((k, rows, columns, width), F32),
            jax.ShapeDtypeStruct((k, k), F32),
        ),
        in_specs=[VMEM, VMEM],
        out_specs=(HBM, VMEM),
        scratch_shapes=[
            pltpu.VMEM((rows, k, columns, width), F32),
            pltpu.SemaphoreType.DMA((2 * rows,)),
        ],
        compiler_params=pltpu.CompilerParams(vmem_limit_bytes=8 << 20),
        name="finish",
    )(sums, placed(field, pltpu.VMEM))


def swap(values, axis, first):
    count = lax.axis_size(axis)
    pairs = []
    for i in range(first, count - 1, 2):
        pairs += [(i, i + 1), (i + 1, i)]
    return lax.ppermute(values, axis, pairs)


def summed(values, axis):
    count = lax.axis_size(axis)
    if count & (count - 1):
        return lax.psum(values, axis)
    bit = 1
    while bit < count:
        values = values + lax.ppermute(values, axis, [(i, i ^ bit) for i in range(count)])
        bit *= 2
    return values


def on_device(start_basis, stiffness, pattern, lumped_mass):
    k, rows, columns, width = start_basis.shape
    flags = jnp.stack([lax.axis_index("sub") % 2, lax.axis_index("dom") % 2]).astype(jnp.int32)
    values = {
        FLAGS: flags,
        STIFFNESS: stiffness,
    }
    made = prepare(flags, start_basis, lumped_mass, jnp.transpose(pattern, (0, 2, 1)))
    values.update(zip((FAR_EDGE, NEAR_EDGE, EVEN, ODD, START, MASS, PATTERN, OUTER), made))
    totals = []
    for level in (1, 2, 3):
        values[FAR_HALO] = swap(values[FAR_EDGE], "sub", 1)
        values[NEAR_HALO] = swap(values[NEAR_EDGE], "sub", 0)
        values[EVEN_SIDE] = swap(values[EVEN], "dom", 0)
        values[ODD_SIDE] = swap(values[ODD], "dom", 1)
        values = level_call(level, INNER, values)
        if level < 3:
            far_corner, near_corner = corners(
                values[MARK], values[EVEN_SIDE], values[ODD_SIDE]
            )
            values[FAR_CORNER] = swap(far_corner, "sub", 1)
            values[NEAR_CORNER] = swap(near_corner, "sub", 0)
        values = level_call(level, NEAR, values)
        values = level_call(level, FAR, values)
        if level > 1:
            totals.append(values[TOTAL])
    sums = jnp.concatenate(totals, axis=1)
    for axis in ("sub", "dom"):
        sums = summed(sums, axis)
    vertex_count = rows * columns * width * lax.axis_size("dom") * lax.axis_size("sub")
    return finish(sums, values[OUTER], rows, columns, 1.0 / vertex_count)


def solution(mesh):
    in_specs = (
        P(None, "sub", "dom", None),
        P("sub", "dom", None, None, None),
        P("sub", "dom", None),
        P("sub", "dom", None),
    )
    out_specs = (P(None, "sub", "dom", None), P())
    return jax.shard_map(
        on_device, mesh=mesh, in_specs=in_specs, out_specs=out_specs, check_vma=False
    )
```

```python
import functools

import jax
import jax.numpy as jnp
from jax import lax
from jax.experimental import pallas as pl
from jax.experimental.pallas import tpu as pltpu
from jax.sharding import PartitionSpec as P

F32 = jnp.float32
BF16 = jnp.bfloat16
LONGEST = 32

VMEM = pl.BlockSpec(memory_space=pltpu.VMEM)
SMEM = pl.BlockSpec(memory_space=pltpu.SMEM)
HBM = pl.BlockSpec(memory_space=pltpu.HBM)


(
    FLAGS, PATTERN, MASS, STIFFNESS, LOADED, OUTER, MIDDLE, TOTAL, FAR_EDGE, NEAR_EDGE, EVEN, ODD,
    MARK, START, LOAD_SEMS, EVEN_SIDE, ODD_SIDE, NEAR_HALO, FAR_HALO, FAR_CORNER,
    NEAR_CORNER,
) = range(21)
INNER, NEAR, FAR = range(3)


def split(values):
    head = values.astype(BF16)
    rest = (values - head.astype(F32)).astype(BF16)
    return jnp.concatenate([head, rest], axis=0)


def joined(pair):
    wide = pair.astype(F32)
    half = wide.shape[0] // 2
    return wide[:half] + wide[half:]


def placed(values, space):
    return pltpu.with_memory_space_constraint(values, space)


def dot_last(left, right):
    return lax.dot_general(left, right, (((1,), (1,)), ((), ())), preferred_element_type=F32)


def folded(square):
    half = square.shape[0] // 2
    rows = square[:half] + square[half:]
    return rows[:, :half] + rows[:, half:]


class Grid:
    def __init__(self, rows, columns, flags=None):
        self.rows, self.columns, self.pitch = rows, columns, columns + 2
        self.blocks = (rows + 2) * self.pitch
        if flags is not None:
            lower, left = flags[0], flags[1]
            self.lower, self.left = lower, left
            self.far_row = lower * (rows - 1)
            self.near_row = (1 - lower) * (rows - 1)
            self.far_halo = lower * (rows + 1)
            self.near_halo = (1 - lower) * (rows + 1)
            self.even_col = (1 - left) * (columns - 1)
            self.odd_col = left * (columns - 1)
            self.even_halo = (1 - left) * (columns + 1)
            self.odd_halo = left * (columns + 1)

    def own(self, row, column):
        return (row + 1) * self.pitch + column + 1

    def padded(self, row, column):
        return row * self.pitch + column

    def slot_rows(self):
        return [self.far_row, self.near_row] + list(range(1, self.rows - 1))


def prepare_kernel(
    rows, columns, flags, start, mass, pattern, far, near, even, odd, middle, held_mass,
    held_pattern, staged, sems
):
    grid = Grid(rows, columns, flags)
    order = grid.slot_rows()
    copies = [
        pltpu.make_async_copy(
            start.at[:, order[slot]],
            staged.at[slot] if slot < 2 else middle.at[slot - 2],
            sems.at[slot],
        )
        for slot in range(rows)
    ] + [
        pltpu.make_async_copy(mass, held_mass, sems.at[rows]),
        pltpu.make_async_copy(pattern, held_pattern, sems.at[rows + 1]),
    ]
    for copy in copies:
        copy.start()
    for slot, edge in ((0, far), (1, near)):
        copies[slot].wait()

        def body(step, _):
            first = pl.multiple_of(step * 8, 8)
            tile = pltpu.einshape("kdr->dkr", staged[slot, :, pl.ds(first, 8), :])
            for inner in range(8):
                edge[step * 8 + inner] = tile[inner]
            return 0

        lax.fori_loop(0, columns // 8, body, 0)
        even[slot] = edge[grid.even_col]
        odd[slot] = edge[grid.odd_col]
    even_right = grid.even_col > 0
    for slot in range(2, rows):
        copies[slot].wait()
        first = pltpu.einshape("kdr->dkr", middle[slot - 2, :, :8, :])[0]
        last = pltpu.einshape("kdr->dkr", middle[slot - 2, :, columns - 8 :, :])[7]
        even[slot] = jnp.where(even_right, last, first)
        odd[slot] = jnp.where(even_right, first, last)
    for copy in copies[rows:]:
        copy.wait()


def prepare(flags, start, mass, pattern):
    k, rows, columns, width = start.shape
    edge = jax.ShapeDtypeStruct((columns, k, width), F32)
    side = jax.ShapeDtypeStruct((rows, k, width), F32)
    return pl.pallas_call(
        functools.partial(prepare_kernel, rows, columns),
        out_shape=(
            edge,
            edge,
            side,
            side,
            pltpu.VMEM((rows - 2, k, columns, width), F32),
            pltpu.VMEM(mass.shape, F32),
            pltpu.VMEM(pattern.shape, jnp.int32),
        ),
        in_specs=[SMEM, HBM, HBM, HBM],
        out_specs=(VMEM,) * 7,
        scratch_shapes=[
            pltpu.VMEM((2, k, columns, width), F32),
            pltpu.SemaphoreType.DMA((rows + 2,)),
        ],
        compiler_params=pltpu.CompilerParams(vmem_limit_bytes=4 << 20),
        name="prepare",
    )(flags, *(placed(values, pltpu.HBM) for values in (start, mass, pattern)))


def corners_kernel(mark, even_side, odd_side, far_corner, near_corner):
    for slot, corner in enumerate((far_corner, near_corner)):
        corner[0] = even_side[slot]
        corner[1] = odd_side[slot]


def corners(mark, even_side, odd_side):
    shape = jax.ShapeDtypeStruct((2,) + even_side.shape[1:], F32)
    return pl.pallas_call(
        corners_kernel,
        out_shape=(shape, shape),
        in_specs=[SMEM, VMEM, VMEM],
        out_specs=(VMEM, VMEM),
        compiler_params=pltpu.CompilerParams(vmem_limit_bytes=1 << 20),
        name="corners",
    )(mark, even_side, odd_side)


def stride_of(count):
    return max(size for size in range(1, LONGEST + 1) if count % size == 0)


def level_kernel(level, part, rows, columns, ref):
    grid = Grid(rows, columns, ref[FLAGS])
    pattern, mass = ref[PATTERN], ref[MASS]
    total = ref.get(TOTAL)
    base = ref[OUTER]
    field = ref[MIDDLE] if level == 2 else ref[OUTER]
    result = {1: ref.get(MIDDLE), 2: ref[OUTER], 3: None}[level]
    stiffness = ref[LOADED] if LOADED in ref else ref[STIFFNESS]
    order = grid.slot_rows()

    loads, ahead = 0, 3
    if LOADED in ref:
        half = columns // 2

        def load(at):
            row = grid.far_row
            if part == INNER:
                row = jnp.where(at // 2 < rows - 2, 1 + at // 2, grid.near_row)
            piece = (row, pl.ds(at % 2 * half, half))
            return pltpu.make_async_copy(
                ref[STIFFNESS].at[piece], ref[LOADED].at[piece], ref[LOAD_SEMS].at[at]
            )

        loads = 2 * rows - 2 if part == INNER else 2
    for at in range(ahead if part == INNER and loads else loads):
        load(at).start()

    def fill(row, blocks):
        def body(step, _):
            for inner in range(8):
                column = step * 8 + inner
                field[grid.padded(row, column + 1)] = split(blocks[column])
            return 0

        lax.fori_loop(0, columns // 8, body, 0)

    if level == 1 and part == INNER:
        fill(grid.far_row + 1, ref[FAR_EDGE])
        fill(grid.near_row + 1, ref[NEAR_EDGE])
        for slot in range(2, rows):

            def relay(step, _):
                first = pl.multiple_of(step * 8, 8)
                values = ref[START][slot - 2, :, pl.ds(first, 8), :]
                tile = pltpu.einshape("kdr->dkr", values)
                for inner in range(8):
                    field[grid.own(order[slot], step * 8 + inner)] = split(tile[inner])
                return 0

            lax.fori_loop(0, columns // 8, relay, 0)
    if part == NEAR:
        for slot, row in enumerate(order):
            field[grid.padded(row + 1, grid.even_halo)] = split(ref[EVEN_SIDE][slot])
            field[grid.padded(row + 1, grid.odd_halo)] = split(ref[ODD_SIDE][slot])
        fill(grid.near_halo, ref[NEAR_HALO])
    if part == (NEAR if level == 3 else FAR):
        for row, name in ((grid.far_halo, FAR_CORNER), (grid.near_halo, NEAR_CORNER)):
            for at, halo in enumerate((grid.even_halo, grid.odd_halo)):
                if level == 3:
                    field[grid.padded(row, halo)] = jnp.zeros(field.shape[1:], BF16)
                else:
                    field[grid.padded(row, halo)] = split(ref[name][at])
    if part == FAR:
        fill(grid.far_halo, ref[FAR_HALO])

    def block(row, column, edge):
        corner = grid.padded(row, column)
        own = grid.own(row, column)
        blocks = [field[own]]
        for slot in range(1, 4):
            offset = pattern[row, slot, column]
            blocks.append(field[corner + offset + (grid.pitch - 3) * ((offset * 11) >> 5)])
        matrix = jnp.concatenate([stiffness[row, column, slot] for slot in range(4)], axis=1)
        products = dot_last(jnp.concatenate(blocks, axis=1), matrix)
        half = products.shape[0] // 2
        coupled = products[:half] + products[half:]
        if level == 3:
            return blocks[0], split(coupled)
        weight = mass[row, pl.ds(column, 1), :]
        scaled = coupled * (1.0 / (3.0 * weight)) - (4.0 / 3.0) * joined(blocks[0])
        if level == 2:
            scaled = 2.0 * scaled - joined(base[own])
        pair = split(scaled)
        result[own] = pair
        if edge is not None:
            edge[column] = scaled
        return (split(scaled * weight), pair) if level == 2 else (None, None)

    def add_terms(terms):
        if level == 1:
            return
        sums = None
        for at in range(0, len(terms), 4):
            lefts, rights = zip(*terms[at : at + 4])
            term = dot_last(jnp.concatenate(lefts, axis=1), jnp.concatenate(rights, axis=1))
            sums = term if sums is None else sums + term
        total[...] += folded(sums)

    def sweep(row, first, count, edge):
        size = stride_of(count)

        def body(step, _):
            add_terms([block(row, first + step * size + at, edge) for at in range(size)])
            return 0

        lax.fori_loop(0, count // size, body, 0)

    near_edge = ref.get(NEAR_EDGE) if level < 3 else None
    if part == INNER:
        ref[MARK][0] = 0
        if level > 1:
            total[...] = jnp.zeros_like(total)
        size = (columns - 2) // 2 if level == 1 else stride_of(columns - 2)
        groups = (columns - 2) // size

        def body(step, _):
            row = 1 + step // groups
            first = 1 + (step % groups) * size
            if loads:
                load(step).wait()

                @pl.when(step + ahead < loads)
                def _():
                    load(step + ahead).start()

            add_terms([block(row, first + at, None) for at in range(size)])
            return 0

        lax.fori_loop(0, (rows - 2) * groups, body, 0)
        if loads:
            for at in range(2 * rows - 4 + ahead, loads):
                load(at).start()
            for at in range(2 * rows - 4, loads):
                load(at).wait()
    ends = (0, columns - 1)
    if part == NEAR:
        first, count = (0, columns) if level == 3 else (1, columns - 2)
        sweep(grid.near_row, first, count, near_edge)
        add_terms([block(row, column, None) for row in order[2:] for column in ends])
        for at in range(loads):
            load(at).wait()
    if part == FAR:
        sweep(grid.far_row, 0, columns, ref.get(FAR_EDGE) if level < 3 else None)
        if level < 3:
            add_terms([block(grid.near_row, column, near_edge) for column in ends])
    if level == 3 and part != INNER:
        slot = rows + (part == NEAR)
        halo = ref[NEAR_HALO] if part == NEAR else ref[FAR_HALO]
        for name, column in ((EVEN_SIDE, grid.even_col), (ODD_SIDE, grid.odd_col)):
            total[...] += folded(dot_last(split(ref[name][slot]), split(halo[column])))
    if level == 2 and part == FAR:
        for slot, row in enumerate(order[:2]):
            down = grid.lower * 2 - 1 if slot == 0 else 1 - grid.lower * 2
            for name, column, right in (
                (EVEN, grid.even_col, 1 - grid.left * 2),
                (ODD, grid.odd_col, grid.left * 2 - 1),
            ):
                across = 3 * (down + 1) + right + 1
                matrix = jnp.zeros(stiffness.shape[3:], BF16)
                for at in range(1, 4):
                    hit = pattern[row, at, column] == across
                    matrix = jnp.where(hit, stiffness[row, column, at], matrix)
                values = jnp.dot(
                    result[grid.own(row, column)], matrix, preferred_element_type=F32
                )
                half = values.shape[0] // 2
                ref[name][rows + slot] = values[:half] + values[half:]
    if level < 3 and part != INNER:
        for slot, row in enumerate(order):
            if (slot < 2) == (part == FAR):
                ref[EVEN][slot] = joined(result[grid.own(row, grid.even_col)])
                ref[ODD][slot] = joined(result[grid.own(row, grid.odd_col)])


def level_call(level, part, values):
    columns, k, width = values[NEAR_EDGE].shape
    rows = values[MASS].shape[0]
    grid = Grid(rows, columns)
    edge = jax.ShapeDtypeStruct((columns, k, width), F32)
    side = jax.ShapeDtypeStruct((rows + 2 * (level == 2), k, width), F32)
    pair = pltpu.VMEM((grid.blocks, 2 * k, width), BF16)
    shapes = {
        OUTER: pair,
        MIDDLE: pair,
        FAR_EDGE: edge,
        NEAR_EDGE: edge,
        EVEN: side,
        ODD: side,
        MARK: jax.ShapeDtypeStruct((1,), jnp.int32),
        TOTAL: jax.ShapeDtypeStruct((k, k), F32),
        LOADED: pltpu.VMEM(values[STIFFNESS].shape, BF16),
    }
    read = [FLAGS, PATTERN, MASS]
    updated, made = [], []
    if level == 1 and part != FAR:
        read.append(STIFFNESS)
        (made if part == INNER else updated).append(LOADED)
    else:
        read.append(LOADED)
    (made if (level, part) == (1, INNER) else updated).extend(
        [OUTER, MIDDLE] if level < 3 else [OUTER]
    )
    if level > 1:
        (made if part == INNER else updated).append(TOTAL)
    scratch = {}
    if part == INNER:
        made.append(MARK)
        if level == 1:
            read += [START, FAR_EDGE, NEAR_EDGE]
            scratch[LOAD_SEMS] = pltpu.SemaphoreType.DMA((2 * rows - 2,))
    elif part == NEAR:
        read += [EVEN_SIDE, ODD_SIDE, NEAR_HALO]
        made += [NEAR_EDGE, EVEN, ODD] if level < 3 else []
        if level == 1:
            scratch[LOAD_SEMS] = pltpu.SemaphoreType.DMA((2,))
    else:
        read.append(FAR_HALO)
        read += [FAR_CORNER, NEAR_CORNER] if level < 3 else [EVEN_SIDE, ODD_SIDE]
        updated += [NEAR_EDGE, EVEN, ODD] if level < 3 else []
        made += [FAR_EDGE] if level < 3 else []
    specs = {FLAGS: SMEM, PATTERN: SMEM, MARK: SMEM, STIFFNESS: HBM}
    spaces = dict.fromkeys((OUTER, MIDDLE, LOADED, MASS, PATTERN, START), pltpu.VMEM)
    spaces.update({STIFFNESS: pltpu.HBM})

    def kernel(*refs):
        skipped = len(read) + len(updated)
        names = read + updated + made + list(scratch)
        ref = dict(zip(names, refs[: len(read)] + refs[skipped:]))
        if LOADED in read:
            ref[STIFFNESS] = ref.pop(LOADED)
        level_kernel(level, part, rows, columns, ref)

    outs = pl.pallas_call(
        kernel,
        out_shape=tuple(shapes[name] for name in updated + made),
        in_specs=[specs.get(name, VMEM) for name in read + updated],
        out_specs=tuple(specs.get(name, VMEM) for name in updated + made),
        scratch_shapes=list(scratch.values()),
        input_output_aliases={len(read) + at: at for at in range(len(updated))},
        compiler_params=pltpu.CompilerParams(vmem_limit_bytes=6 << 20),
        name=("inner", "near", "far")[part],
    )(*[placed(values[name], spaces[name]) if name in spaces else values[name]
        for name in read + updated])
    return {**values, **dict(zip(updated + made, outs))}


def inverse_factor(gram):
    k, step = gram.shape[0], 8
    lines = lax.broadcasted_iota(jnp.int32, (k, 2 * k), 0)
    lanes = lax.broadcasted_iota(jnp.int32, (k, 2 * k), 1)
    work = jnp.concatenate([gram, (lines == lanes).astype(F32)[:, :k]], axis=1)
    finished = []
    for first in range(0, k, step):
        rows = [work[at : at + 1] for at in range(step)]
        columns = [
            jnp.broadcast_to(work[:, first + at : first + at + 1], work.shape)
            for at in range(step)
        ]
        entries = [
            [jnp.broadcast_to(rows[i][:, first + j : first + j + 1], (1, 2 * k)) for j in range(step)]
            for i in range(step)
        ]
        change = None
        for i in range(step):
            scale = 1.0 / entries[i][i]
            line = rows[i] * scale
            for j in range(i + 1, step):
                factor = entries[i][j] * scale
                for t in range(j, step):
                    entries[j][t] = entries[j][t] - factor * entries[i][t]
                rows[j] = rows[j] - factor * rows[i]
                columns[j] = columns[j] - columns[i] * factor
            column = jnp.where(lines[:step] > i, columns[i][:step], 0.0)
            if work.shape[0] > step:
                column = jnp.concatenate([column, columns[i][step:]], axis=0)
            change = column * line if change is None else change + column * line
        work = work - change
        finished.append(work[:step])
        work = work[step:]
    work = jnp.concatenate(finished, axis=0)
    pivots = jnp.sum(jnp.where(lines == lanes, work, 0.0), axis=1, keepdims=True)
    return work[:, k:] * lax.rsqrt(pivots)


def finish_kernel(rows, columns, inverse_count, sums, field, out, projected, staged, sems):
    k = projected.shape[0]
    grid = Grid(rows, columns)
    highest = lax.Precision.HIGHEST
    inverse = inverse_factor(sums[:, :k] * inverse_count)
    parts = split(inverse)
    left = jnp.concatenate([parts, parts], axis=1)
    half = columns // 2

    def copy(row, side):
        piece = pl.ds(side * half, half)
        return pltpu.make_async_copy(
            staged.at[row, :, piece], out.at[:, row, piece], sems.at[2 * row + side]
        )

    def body(step, _):
        row, side = step // 2, step % 2
        for tile in range(0, half, 8):
            first = pl.multiple_of(side * half + tile, 8)
            blocks = []
            for at in range(8):
                both = jnp.dot(left, field[grid.own(row, first + at)], preferred_element_type=F32)
                blocks.append((both[:k] + both[k:])[None])
            staged[row, :, pl.ds(first, 8), :] = pltpu.einshape(
                "dkr->kdr", jnp.concatenate(blocks, axis=0)
            )
        copy(row, side).start()
        return 0

    lax.fori_loop(0, 2 * rows, body, 0)
    moments = sums[:, k:] * inverse_count
    partial = jnp.dot(inverse, moments, precision=highest, preferred_element_type=F32)
    projected[...] = lax.dot_general(
        partial, inverse, (((1,), (1,)), ((), ())), precision=highest, preferred_element_type=F32
    )
    for step in range(2 * rows):
        copy(step // 2, step % 2).wait()


def finish(sums, field, rows, columns, inverse_count):
    k = sums.shape[0]
    width = field.shape[2]
    return pl.pallas_call(
        functools.partial(finish_kernel, rows, columns, inverse_count),
        out_shape=(
            jax.ShapeDtypeStruct((k, rows, columns, width), F32),
            jax.ShapeDtypeStruct((k, k), F32),
        ),
        in_specs=[VMEM, VMEM],
        out_specs=(HBM, VMEM),
        scratch_shapes=[
            pltpu.VMEM((rows, k, columns, width), F32),
            pltpu.SemaphoreType.DMA((2 * rows,)),
        ],
        compiler_params=pltpu.CompilerParams(vmem_limit_bytes=8 << 20),
        name="finish",
    )(sums, placed(field, pltpu.VMEM))


def swap(values, axis, first):
    count = lax.axis_size(axis)
    pairs = []
    for i in range(first, count - 1, 2):
        pairs += [(i, i + 1), (i + 1, i)]
    return lax.ppermute(values, axis, pairs)


def summed(values, axis):
    count = lax.axis_size(axis)
    if count & (count - 1):
        return lax.psum(values, axis)
    bit = 1
    while bit < count:
        values = values + lax.ppermute(values, axis, [(i, i ^ bit) for i in range(count)])
        bit *= 2
    return values


def on_device(start_basis, stiffness, pattern, lumped_mass):
    k, rows, columns, width = start_basis.shape
    flags = jnp.stack([lax.axis_index("sub") % 2, lax.axis_index("dom") % 2]).astype(jnp.int32)
    values = {
        FLAGS: flags,
        STIFFNESS: stiffness,
    }
    made = prepare(flags, start_basis, lumped_mass, jnp.transpose(pattern, (0, 2, 1)))
    values.update(zip((FAR_EDGE, NEAR_EDGE, EVEN, ODD, START, MASS, PATTERN), made))
    totals = []
    for level in (1, 2, 3):
        values[FAR_HALO] = swap(values[FAR_EDGE], "sub", 1)
        values[NEAR_HALO] = swap(values[NEAR_EDGE], "sub", 0)
        values[EVEN_SIDE] = swap(values[EVEN], "dom", 0)
        values[ODD_SIDE] = swap(values[ODD], "dom", 1)
        values = level_call(level, INNER, values)
        if level < 3:
            far_corner, near_corner = corners(
                values[MARK], values[EVEN_SIDE], values[ODD_SIDE]
            )
            values[FAR_CORNER] = swap(far_corner, "sub", 1)
            values[NEAR_CORNER] = swap(near_corner, "sub", 0)
        values = level_call(level, NEAR, values)
        values = level_call(level, FAR, values)
        if level > 1:
            totals.append(values[TOTAL])
    sums = jnp.concatenate(totals, axis=1)
    for axis in ("sub", "dom"):
        sums = summed(sums, axis)
    vertex_count = rows * columns * width * lax.axis_size("dom") * lax.axis_size("sub")
    return finish(sums, values[OUTER], rows, columns, 1.0 / vertex_count)


def solution(mesh):
    in_specs = (
        P(None, "sub", "dom", None),
        P("sub", "dom", None, None, None),
        P("sub", "dom", None),
        P("sub", "dom", None),
    )
    out_specs = (P(None, "sub", "dom", None), P())
    return jax.shard_map(
        on_device, mesh=mesh, in_specs=in_specs, out_specs=out_specs, check_vma=False
    )
```
